256 devices in a mesh: half: 2 (over core), rows: 128 (over y, x, z).
Axes of the slice: x: 4, y: 4, z: 8, core: 2. Of those that a mesh axis runs over, the one named last changes fastest.
Arguments:
- factors: float32 [2, 131072, 256], P('half', 'rows'), may hold values from -8 to 8
- coefficients: float32 [256, 256], replicated, may hold values from -1 to 9
- density: float32 [131072], P('rows'), may hold values from 0.25 to 4
Outputs:
- new_factors: float32 [2, 131072, 256], P('half', 'rows')
- new_coefficients: float32 [256, 256], P('half')
The draws below stay inside these ranges and needn't reach their ends.
All inputs are finite; a program needn't handle non-finite values.
Results may differ from the reference program's by a relative error of at most 0.0001.
Values sent between devices are 32-bit elements; how exact they have to be, the bound alone decides.
No kernel may reach another device: no remote copies, remote signals or barrier semaphores. Data moves between devices by JAX's collectives and lax.ppermute only.
A program may use at most 128 MiB of HBM per device.

```python
import jax
import jax.numpy as jnp
from jax import lax

R = 256
NY = 32
NZ = 32
VGRID = 64
NR = 131072
NX = 128


def density_values(key):
    return jnp.exp(jax.random.uniform(jax.random.fold_in(key, 37), (NR,), jnp.float32, -1.3862944, 1.3862944))


def draw_density(key, part):
    return density_values(key)


def draw_factors(key, part):
    first_key, second_key = jax.random.split(jax.random.fold_in(key, 11))
    space_factor = jnp.clip(jax.random.normal(first_key, (NR, R), jnp.float32), -6.0, 6.0)
    velocity_factor = jnp.clip(jax.random.normal(second_key, (NR, R), jnp.float32), -6.0, 6.0)
    cell_density = density_values(key)
    density_column = cell_density / jnp.sqrt(jnp.mean(cell_density * cell_density))
    space_factor = space_factor.at[:, 0].set(density_column + 0.4 * space_factor[:, 0])
    last_points = NR // (VGRID * VGRID)
    row_index = jnp.arange(NR, dtype=jnp.int32)
    third_index = row_index % last_points
    second = row_index // last_points % VGRID
    first_index = row_index // (last_points * VGRID)
    speeds = jnp.stack([-1.0 + (2 * first_index + 1).astype(jnp.float32) / VGRID, -1.0 + (2 * second + 1).astype(jnp.float32) / VGRID, -1.0 + (2 * third_index + 1).astype(jnp.float32) / last_points])
    maxwell = jnp.exp(-2.0 * jnp.sum(speeds * speeds, axis=0))
    column = maxwell / jnp.sqrt(jnp.mean(maxwell * maxwell))
    velocity_factor = velocity_factor.at[:, 0].set(column + 0.4 * velocity_factor[:, 0])
    return jnp.stack([space_factor, velocity_factor])


def draw_coefficients(key, part):
    first_key, second_key = jax.random.split(jax.random.fold_in(key, 23))
    diagonal = jnp.exp(jax.random.uniform(first_key, (R,), jnp.float32, 0.6931472, 2.0794415))
    noise = jnp.clip(jax.random.normal(second_key, (R, R), jnp.float32), -6.0, 6.0)
    return jnp.diag(diagonal) + 0.5 / jnp.sqrt(float(R)) * noise


def setup_inputs(seed: int = 0) -> dict:
    keys = jax.random.split(jax.random.key(seed), 4)
    return {
        "factors": draw_factors(jax.random.fold_in(keys[3], 71), 0),
        "coefficients": draw_coefficients(jax.random.fold_in(keys[3], 71), 0),
        "density": draw_density(jax.random.fold_in(keys[3], 71), 0),
    }


time_step = 0.2
relax_time = 0.5

def project(left, right, total_rows):
    return lax.dot_general(left.astype(jnp.float32), right.astype(jnp.float32), (((0,), (0,)), ((), ())), precision=lax.Precision.HIGHEST, preferred_element_type=jnp.float32) / total_rows

def matmul(left, right):
    return jnp.dot(left.astype(jnp.float32), right.astype(jnp.float32), precision=lax.Precision.HIGHEST, preferred_element_type=jnp.float32)

def velocity_grid(start, row_count, total_rows):
    last_points = total_rows // (VGRID * VGRID)
    row_index = start + jnp.arange(row_count, dtype=jnp.int32)
    third_index = row_index % last_points
    second = row_index // last_points % VGRID
    first_index = row_index // (last_points * VGRID)
    speeds = jnp.stack([-1.0 + (2 * first_index + 1).astype(jnp.float32) / VGRID, -1.0 + (2 * second + 1).astype(jnp.float32) / VGRID, -1.0 + (2 * third_index + 1).astype(jnp.float32) / last_points])
    maxwell = jnp.exp(-2.0 * jnp.sum(speeds * speeds, axis=0))
    return (speeds, maxwell)

def grid_slopes(values):
    width = values.shape[3]
    slopes = []
    for axis_index in range(3):
        minus_part = values - jnp.roll(values, 1, axis_index)
        plus_part = jnp.roll(values, -1, axis_index) - values
        slopes.append((minus_part.reshape(-1, width), plus_part.reshape(-1, width)))
    return slopes

def space_moments(local_factor, slopes, density, total_rows):
    matrices = [project(local_factor, pair[0], total_rows) for pair in slopes]
    matrices = matrices + [project(local_factor, pair[1], total_rows) for pair in slopes]
    return (jnp.stack(matrices), project(local_factor, density[:, None], total_rows)[:, 0])

def velocity_moments(local_factor, speeds, maxwell, total_rows):
    plus_speed = jnp.maximum(speeds, 0.0)
    minus_speed = jnp.minimum(speeds, 0.0)
    matrices = [project(local_factor, plus_speed[k][:, None] * local_factor, total_rows) for k in range(3)]
    matrices = matrices + [project(local_factor, minus_speed[k][:, None] * local_factor, total_rows) for k in range(3)]
    return (jnp.stack(matrices), project(local_factor, maxwell[:, None], total_rows)[:, 0])

def space_update(local_factor, slopes, coefficients, velocity_set, density):
    matrices, vector = velocity_set
    product = matmul(local_factor, coefficients)
    transport = jnp.zeros_like(product)
    for direction in range(3):
        transport = transport + matmul(slopes[direction][0], matmul(coefficients, matrices[direction]))
        transport = transport + matmul(slopes[direction][1], matmul(coefficients, matrices[3 + direction]))
    return product - time_step * transport + time_step / relax_time * (density[:, None] * vector[None, :] - product)

def velocity_update(local_factor, speeds, maxwell, coefficients, space_set):
    matrices, vector = space_set
    plus_speed = jnp.maximum(speeds, 0.0)
    minus_speed = jnp.minimum(speeds, 0.0)
    product = matmul(local_factor, coefficients.T)
    transport = jnp.zeros_like(product)
    for direction in range(3):
        transport = transport + plus_speed[direction][:, None] * matmul(product, matrices[direction].T)
        transport = transport + minus_speed[direction][:, None] * matmul(product, matrices[3 + direction].T)
    return product - time_step * transport + time_step / relax_time * (maxwell[:, None] * vector[None, :] - product)

def from_lower(values, lower_factor):
    identity = jnp.eye(lower_factor.shape[0], dtype=jnp.float32)
    inverse = jax.scipy.linalg.solve_triangular(lower_factor, identity, lower=True)
    return matmul(values, inverse.T)

def coefficient_step(coefficients, space_set, velocity_set):
    space_mats, space_vector = space_set
    velocity_mats, velocity_vector = velocity_set
    galerkin = matmul(matmul(space_mats[0], coefficients), velocity_mats[0].T)
    transport = jnp.zeros_like(galerkin)
    for direction in range(3):
        transport = transport + matmul(matmul(space_mats[1 + direction], galerkin), velocity_mats[1 + direction])
        transport = transport + matmul(matmul(space_mats[4 + direction], galerkin), velocity_mats[4 + direction])
    return galerkin - time_step * transport + time_step / relax_time * (space_vector[:, None] * velocity_vector[None, :] - galerkin)

def reference(factors, coefficients, density):
    space_factor = factors[0]
    velocity_factor = factors[1]
    speeds, maxwell = velocity_grid(0, NR, NR)
    slopes = grid_slopes(space_factor.reshape(NX, NY, NZ, R))
    space_set = space_moments(space_factor, slopes, density, NR)
    velocity_set = velocity_moments(velocity_factor, speeds, maxwell, NR)
    k_field = space_update(space_factor, slopes, coefficients, velocity_set, density)
    l_field = velocity_update(velocity_factor, speeds, maxwell, coefficients, space_set)
    space_basis = from_lower(k_field, jnp.linalg.cholesky(project(k_field, k_field, NR)))
    velocity_basis = from_lower(l_field, jnp.linalg.cholesky(project(l_field, l_field, NR)))
    new_slopes = grid_slopes(space_basis.reshape(NX, NY, NZ, R))
    space_mats, space_vector = space_moments(space_basis, new_slopes, density, NR)
    space_two = (jnp.concatenate([project(space_basis, space_factor, NR)[None], space_mats]), space_vector)
    velocity_mats, velocity_vector = velocity_moments(velocity_basis, speeds, maxwell, NR)
    velocity_two = (jnp.concatenate([project(velocity_basis, velocity_factor, NR)[None], velocity_mats]), velocity_vector)
    updated = coefficient_step(coefficients, space_two, velocity_two)
    return (jnp.stack([space_basis, velocity_basis]), updated)
```

```python
import functools

import jax
import jax.numpy as jnp
from jax import lax
from jax.experimental import pallas as pl
from jax.experimental.pallas import tpu as pltpu
from jax.sharding import Mesh
from jax.sharding import PartitionSpec as P

NY = 32
NZ = 32
VGRID = 64
R = 256
H = R // 2
AXES = ("y", "x", "z")
PLANE = ("y", "x")
CELLS = ("half", "y", "x", "z")

time_step = 0.2
relax_time = 0.5
KEEP = 1.0 - time_step / relax_time
GAIN = time_step / relax_time


def dot(a, b, ca=1, cb=0):
    return lax.dot_general(
        a,
        b,
        (((ca,), (cb,)), ((), ())),
        precision=lax.Precision.HIGHEST,
        preferred_element_type=jnp.float32,
    )


def split(x):
    high = x.astype(jnp.bfloat16)
    return high, (x - high.astype(jnp.float32)).astype(jnp.bfloat16)


def dot3(a, b, ca=1, cb=0):
    def part(x, y):
        return lax.dot_general(
            x, y, (((ca,), (cb,)), ((), ())), preferred_element_type=jnp.float32
        )

    return part(a[0], b[0]) + (part(a[0], b[1]) + part(a[1], b[0]))


def plane_scatter(x):
    size = lax.axis_size(PLANE)
    parts = x.reshape(size, x.shape[0] // size, x.shape[1])
    return lax.all_to_all(parts, PLANE, 0, 0, tiled=True).sum(axis=0)


def plane_gather(part):
    size = lax.axis_size(PLANE)
    parts = lax.all_to_all(
        jnp.broadcast_to(part[None], (size, *part.shape)), PLANE, 0, 0, tiled=True
    )
    return parts.reshape(size * part.shape[0], part.shape[1])


def line_total(x):
    size = lax.axis_size("z")
    step = 1
    while step < size:
        x = x + lax.ppermute(x, "z", [(i, i ^ step) for i in range(size)])
        step *= 2
    return x


def swap_halves(x):
    return lax.ppermute(x, "half", [(0, 1), (1, 0)])


def to_neighbour(x, distance):
    count = lax.axis_size(AXES)
    return lax.ppermute(x, CELLS, [(i, (i + distance) % count) for i in range(count)])


def whole(count):
    return [pl.BlockSpec(memory_space=pltpu.VMEM)] * count


def kernel_call(body, name, out, arrays, meta, scratch=()):
    outs = out if isinstance(out, list) else [out]
    results = pl.pallas_call(
        body,
        out_shape=[jax.ShapeDtypeStruct(shape, jnp.float32) for shape in outs],
        in_specs=[pl.BlockSpec(memory_space=pltpu.SMEM)] + whole(len(arrays)),
        out_specs=whole(len(outs)),
        scratch_shapes=list(scratch),
        name=name,
    )(meta, *arrays)
    return results if isinstance(out, list) else results[0]


B = 64


def block_inverse(d, out_ref):
    rows = lax.broadcasted_iota(jnp.int32, (B, B), 0)
    cols = lax.broadcasted_iota(jnp.int32, (B, B), 1)
    eye = jnp.where(rows == cols, 1.0, 0.0).astype(jnp.float32)
    wide = jnp.concatenate([d, eye], axis=1)
    blk = [wide[8 * i : 8 * i + 8, :] for i in range(B // 8)]
    sub = lax.broadcasted_iota(jnp.int32, (8, 2 * B), 0)

    def lane(v, j):
        return jnp.broadcast_to(v[:, j : j + 1], (8, 2 * B))

    def row(v, s):
        return jnp.broadcast_to(v[s : s + 1, :], (8, 2 * B))

    for j in range(0, B, 2):
        jb, s = j // 8, j % 8
        c0 = [lane(blk[i], j) for i in range(jb, B // 8)]
        c1 = [lane(blk[i], j + 1) for i in range(jb, B // 8)]
        p00, p01, p11 = row(c0[0], s), row(c1[0], s), row(c1[0], s + 1)
        r0, r1 = row(blk[jb], s), row(blk[jb], s + 1)
        inv = 1.0 / (p00 * p11 - p01 * p01)
        w0 = (p11 * r0 - p01 * r1) * inv
        w1 = (p00 * r1 - p01 * r0) * inv
        ratio = p01 / p00
        o0 = r0 * (1.0 / jnp.sqrt(p00))
        o1 = (r1 - ratio * r0) * (1.0 / jnp.sqrt(p11 - ratio * p01))
        both = jnp.where(sub == s, o0, o1)
        out_ref[j : j + 2, :] = both[s : s + 2, B:]
        for i in range(jb, B // 8):
            change = c0[i - jb] * w0 + c1[i - jb] * w1
            if i == jb:
                change = jnp.where(sub > s + 1, change, 0.0)
            blk[i] = blk[i] - change


def inverse_factor_body(meta, sums_ref, out_ref, work, small):
    rows = lax.broadcasted_iota(jnp.int32, (R, R), 0)
    cols = lax.broadcasted_iota(jnp.int32, (R, R), 1)
    work[:H, :] = sums_ref[:H, :]
    work[H:, :H] = sums_ref[:H, H:].T
    work[H:, H:] = sums_ref[H:R, H:]
    g = work[...]
    diag = jnp.where(rows == cols, g, 0.0)
    across = 1.0 / jnp.sqrt(jnp.sum(diag, axis=0, keepdims=True))
    down = 1.0 / jnp.sqrt(jnp.sum(diag, axis=1, keepdims=True))
    work[...] = g * across * down
    for k in range(R // B):
        lo, hi = k * B, (k + 1) * B
        block_inverse(work[lo:hi, lo:hi], small)
        ik = small[...]
        left = dot(ik, work[lo:hi, :])
        ccols = lax.broadcasted_iota(jnp.int32, (B, R), 1)
        wide = jnp.concatenate([ik] * (R // B), axis=1)
        panel = jnp.where((ccols >= lo) & (ccols < hi), wide, left)
        work[lo:hi, :] = panel
        if hi < R:
            update = dot(left, panel, 0, 0)
            below = work[hi:, :]
            bcols = lax.broadcasted_iota(jnp.int32, (R - hi, R), 1)
            below = jnp.where((bcols >= lo) & (bcols < hi), 0.0, below)
            work[hi:, :] = below - update[hi:, :]
    out_ref[...] = jnp.where(rows >= cols, work[...], 0.0) * across


def upper_mask():
    return lax.broadcasted_iota(jnp.int32, (R, R), 0) <= lax.broadcasted_iota(jnp.int32, (R, R), 1)


def diagonal_mask():
    return lax.broadcasted_iota(jnp.int32, (R, R), 0) == lax.broadcasted_iota(jnp.int32, (R, R), 1)


def shifted_y(x, forward):
    if forward:
        return jnp.concatenate([x[NZ:], x[:NZ]], axis=0)
    return jnp.concatenate([x[-NZ:], x[:-NZ]], axis=0)


def shifted_z(x, forward):
    count = x.shape[0]
    place = lax.broadcasted_iota(jnp.int32, x.shape, 0) & (NZ - 1)
    if forward:
        return jnp.where(
            place == NZ - 1, pltpu.roll(x, NZ - 1, 0), pltpu.roll(x, count - 1, 0)
        )
    return jnp.where(place == 0, pltpu.roll(x, count - NZ + 1, 0), pltpu.roll(x, 1, 0))


def grid_speeds(meta, count, width):
    start = meta[1]
    row = lax.broadcasted_iota(jnp.int32, (count, width), 0)
    third = (row & (NZ - 1)).astype(jnp.float32)
    second = ((start // NZ) % VGRID + row // NZ).astype(jnp.float32)
    first = (start // (NZ * VGRID)).astype(jnp.float32)
    v0 = -1.0 + (2.0 * first + 1.0) / VGRID
    v1 = -1.0 + (2.0 * second + 1.0) / VGRID
    v2 = -1.0 + (2.0 * third + 1.0) / NZ
    maxwell = jnp.exp(-2.0 * (v0 * v0 + v1 * v1 + v2 * v2))
    return v0, v1, v2, maxwell


def first_sign(meta):
    return meta[1] // (NZ * VGRID) >= VGRID // 2


def second_sign(meta):
    return (meta[1] // NZ) % VGRID >= VGRID // 2


def unpack_speed(packed, diag):
    upper, diagonal = upper_mask(), diagonal_mask()
    flipped = packed.T
    plus = jnp.where(upper, packed, flipped)
    minus = jnp.where(diagonal, diag, jnp.where(upper, flipped, packed))
    return plus, minus


def put_speed_sums(meta, f, turned, gram, scale, out_ref, at, put_vector):
    upper, diagonal = upper_mask(), diagonal_mask()
    v0, v1, v2, maxwell = grid_speeds(meta, f.shape[0], R)

    def one_sign(d, value, positive):
        low = jnp.where(upper, 0.0, value)
        high = jnp.where(upper, value, 0.0)
        out_ref[at + d * R : at + (d + 1) * R, :] = jnp.where(positive, high, low)
        diag = jnp.where(diagonal, value, 0.0).sum(axis=0, keepdims=True)
        put_vector(d + 1, jnp.where(positive, 0.0, diag))

    one_sign(0, v0 * gram, first_sign(meta))
    one_sign(1, dot3(turned, split(v1 * f)) * scale, second_sign(meta))
    plus = dot3(turned, split(jnp.maximum(v2, 0.0) * f)) * scale
    minus = dot3(turned, split(jnp.minimum(v2, 0.0) * f)) * scale
    out_ref[at + 2 * R : at + 3 * R, :] = jnp.where(upper, plus, minus)
    put_vector(3, jnp.where(diagonal, minus, 0.0).sum(axis=0, keepdims=True))
    put_vector(0, (f * maxwell).sum(axis=0, keepdims=True) * scale)


def first_body(total, meta, f_ref, density_ref, out_ref):
    scale = 1.0 / total
    out_ref[3 * R :, :] = jnp.zeros((out_ref.shape[0] - 3 * R, R), jnp.float32)

    def put_vector(k, value):
        out_ref[3 * R + k : 3 * R + k + 1, :] = value

    f = f_ref[...]
    turned = split(f.T)

    @pl.when(meta[0] == 0)
    def _():
        out_ref[:R, :] = jnp.zeros((R, R), jnp.float32)
        out_ref[R : 2 * R, :] = dot3(turned, split(shifted_y(f, True) - f)) * scale
        out_ref[2 * R : 3 * R, :] = dot3(turned, split(shifted_z(f, True) - f)) * scale
        put_vector(0, (f * density_ref[...]).sum(axis=0, keepdims=True) * scale)

    @pl.when(meta[0] == 1)
    def _():
        put_speed_sums(meta, f, turned, dot3(turned, split(f)) * scale, scale, out_ref, 0, put_vector)


def across_body(at, total, meta, *refs):
    *parts, following_ref, previous_ref, sums_ref, out_ref, block, sem = refs
    del sums_ref

    @pl.when(meta[0] == 0)
    def _():
        if len(parts) == 1:
            half = parts[0].shape[0] // 2
            low, high = parts[0][:half, :], parts[0][half:, :]
        else:
            low, high = parts[0][...], parts[1][...]
        half = low.shape[0]
        following = following_ref[:half, :]
        previous = previous_ref[previous_ref.shape[0] - half :, :]
        left = jnp.concatenate([low, previous], axis=0)
        right = jnp.concatenate([following - low, high - previous], axis=0)
        block[...] = dot3(split(left.T), split(right)) * (1.0 / total)
        copy = pltpu.make_async_copy(block, out_ref.at[pl.ds(at, R), :], sem)
        copy.start()
        copy.wait()


def add_across(at, total, parts, following, previous, sums, meta):
    count = len(parts) + 2
    return pl.pallas_call(
        functools.partial(across_body, at, total),
        out_shape=jax.ShapeDtypeStruct(sums.shape, jnp.float32),
        in_specs=[pl.BlockSpec(memory_space=pltpu.SMEM)]
        + whole(count)
        + [pl.BlockSpec(memory_space=pl.ANY)],
        out_specs=pl.BlockSpec(memory_space=pl.ANY),
        scratch_shapes=[pltpu.VMEM((R, R), jnp.float32), pltpu.SemaphoreType.DMA(())],
        input_output_aliases={count + 1: 0},
        name="across",
    )(meta, *parts, following, previous, sums)


def next_body(
    meta, f_ref, following_ref, previous_ref, theirs_ref, s_ref, density_ref, low_ref, high_ref
):
    half = low_ref.shape[0]

    def vector(k):
        return theirs_ref[3 * R + k : 3 * R + k + 1, :]

    def matrix(d):
        return theirs_ref[d * R : (d + 1) * R, :]

    def put(value):
        low_ref[...] = value[:half, :]
        high_ref[...] = value[half:, :]

    @pl.when(meta[0] == 0)
    def _():
        f = f_ref[...]
        s = split(s_ref[...])
        out = dot3(split(f), split(KEEP * s_ref[...])) + GAIN * (density_ref[...] * vector(0))
        for d in range(3):
            plus, minus = unpack_speed(matrix(d), vector(d + 1))
            back = (previous_ref[...], shifted_y(f, False), shifted_z(f, False))[d]
            ahead = (following_ref[...], shifted_y(f, True), shifted_z(f, True))[d]
            change = dot3(split(f - back), split(dot3(s, split(plus))))
            change = change + dot3(split(ahead - f), split(dot3(s, split(minus))))
            out = out - time_step * change
        put(out)

    @pl.when(meta[0] == 1)
    def _():
        v0, v1, v2, maxwell = grid_speeds(meta, f_ref.shape[0], R)
        l = dot3(split(f_ref[...]), split(s_ref[...]), 1, 1)
        parts = split(l)
        out = KEEP * l + GAIN * (maxwell * vector(0))
        for d, v, positive in ((0, v0, first_sign(meta)), (1, v1, second_sign(meta))):
            e = matrix(d)
            out = out - time_step * (v * dot3(parts, split(jnp.where(positive, -e, e.T))))
        e = split(matrix(2))
        out = out + time_step * (jnp.maximum(v2, 0.0) * dot3(parts, e))
        put(out - time_step * (jnp.minimum(v2, 0.0) * dot3(parts, e, 1, 1)))


def second_body(total, meta, low_ref, high_ref, f_ref, density_ref, out_ref):
    scale = 1.0 / total
    k = jnp.concatenate([low_ref[...], high_ref[...]], axis=0)
    straight = k.T
    gram = dot(straight, k) * scale
    turned = split(straight)
    out_ref[:H, :] = gram[:H, :]
    out_ref[H:R, :H] = jnp.zeros((H, H), jnp.float32)
    out_ref[H:R, H:] = gram[H:, H:]
    out_ref[R : 2 * R, :] = dot3(turned, split(f_ref[...])) * scale

    def put_vector(i, value):
        out_ref[H + 2 * i : H + 2 * i + 1, :H] = value[:, :H]
        out_ref[H + 2 * i + 1 : H + 2 * i + 2, :H] = value[:, H:]

    @pl.when(meta[0] == 0)
    def _():
        out_ref[2 * R : 3 * R, :] = jnp.zeros((R, R), jnp.float32)
        out_ref[3 * R : 4 * R, :] = dot3(turned, split(shifted_y(k, True) - k)) * scale
        out_ref[4 * R : 5 * R, :] = dot3(turned, split(shifted_z(k, True) - k)) * scale
        put_vector(0, (k * density_ref[...]).sum(axis=0, keepdims=True) * scale)

    @pl.when(meta[0] == 1)
    def _():
        put_speed_sums(meta, k, turned, gram, scale, out_ref, 2 * R, put_vector)


def basis_body(meta, low_ref, high_ref, inverse_ref, out_ref):
    half = low_ref.shape[0]
    inverse = inverse_ref[...].T
    out_ref[:half, :] = dot(low_ref[...], inverse)
    out_ref[half:, :] = dot(high_ref[...], inverse)


def coefficient_body(meta, mine_ref, other_ref, inverse_ref, other_inverse_ref, s_ref, out_ref):
    def work(half, space_ref, speed_ref, pk_ref, pv_ref):
        def vector(ref, k):
            at = H + 2 * k
            return jnp.concatenate([ref[at : at + 1, :H], ref[at + 1 : at + 2, :H]], axis=1)

        pk, pv = pk_ref[...], pv_ref[...]
        rows = pk[half * H : (half + 1) * H, :]
        middle = dot(dot(space_ref[R : 2 * R, :], s_ref[...]), speed_ref[R : 2 * R, :], 1, 1)
        z = dot(dot(pk, dot(pk, middle), 0, 0), dot(pv, pv, 0, 0))
        parts = []
        for d in range(3):
            h = space_ref[(2 + d) * R : (3 + d) * R, :]
            parts += [dot(rows, h), dot(rows, h, 1, 1)]
        parts = dot(jnp.concatenate(parts, axis=0), z)
        change = jnp.zeros((H, R), jnp.float32)
        for d in range(3):
            packed = speed_ref[(2 + d) * R : (3 + d) * R, :]
            plus, minus = unpack_speed(packed, vector(speed_ref, d + 1))
            change = change + dot(parts[2 * d * H : (2 * d + 1) * H, :], minus)
            change = change - dot(parts[(2 * d + 1) * H : (2 * d + 2) * H, :], plus)
        xb = jnp.sum(rows * vector(space_ref, 0), axis=1, keepdims=True)
        out = KEEP * dot(rows, middle) - time_step * change + GAIN * (xb * vector(speed_ref, 0))
        out_ref[...] = dot(out, pv, 1, 1)

    @pl.when(meta[0] == 0)
    def _():
        work(0, mine_ref, other_ref, inverse_ref, other_inverse_ref)

    @pl.when(meta[0] == 1)
    def _():
        work(1, other_ref, mine_ref, other_inverse_ref, inverse_ref)


def local(factors, coefficients, density):
    rows_here = factors.shape[1]
    total = rows_here * lax.axis_size(AXES)
    start = lax.axis_index(AXES) * rows_here
    meta = jnp.stack([lax.axis_index("half"), start]).astype(jnp.int32)
    f = factors[0]
    column = density[:, None]

    following = to_neighbour(f, -1)
    previous = to_neighbour(f, 1)

    sums = kernel_call(
        functools.partial(first_body, total), "first_sums", (3 * R + 128, R), [f, column], meta
    )
    sums = add_across(0, total, [f], following, previous, sums, meta)
    theirs = plane_gather(swap_halves(line_total(plane_scatter(sums))))
    low, high = kernel_call(
        next_body,
        "next_factor",
        [(rows_here // 2, R)] * 2,
        [f, following, previous, theirs, coefficients, column],
        meta,
    )

    next_low = to_neighbour(low, -1)
    last_high = to_neighbour(high, 1)
    sums = kernel_call(
        functools.partial(second_body, total), "second_sums", (5 * R, R), [low, high, f, column], meta
    )
    sums = add_across(2 * R, total, [low, high], next_low, last_high, sums, meta)
    mine = plane_gather(line_total(plane_scatter(sums)))
    other = swap_halves(mine)
    inverse = kernel_call(
        inverse_factor_body,
        "inverse_factor",
        (R, R),
        [mine],
        meta,
        scratch=[pltpu.VMEM((R, R), jnp.float32), pltpu.VMEM((B, B), jnp.float32)],
    )
    other_inverse = swap_halves(inverse)
    basis = kernel_call(basis_body, "basis", (rows_here, R), [low, high, inverse], meta)
    updated = kernel_call(
        coefficient_body,
        "coefficients",
        (H, R),
        [mine, other, inverse, other_inverse, coefficients],
        meta,
    )
    return (basis[None], updated)


def solution(mesh):
    torus = Mesh(mesh.devices.reshape(mesh.shape["half"], 4, 4, 8), CELLS)
    return jax.shard_map(
        local,
        mesh=torus,
        in_specs=(P("half", AXES, None), P(), P(AXES)),
        out_specs=(P("half", AXES, None), P("half", None)),
        check_vma=False,
    )
```

```python
import functools

import jax
import jax.numpy as jnp
from jax import lax
from jax.experimental import pallas as pl
from jax.experimental.pallas import tpu as pltpu
from jax.sharding import Mesh
from jax.sharding import PartitionSpec as P

NZ = 32
VGRID = 64
R = 256
H = R // 2
AXES = ("y", "x", "zh", "zl")
PLANE = ("y", "x", "zl")
CELLS = ("half", "y", "x", "zh", "zl")

time_step = 0.2
relax_time = 0.5
KEEP = 1.0 - time_step / relax_time
GAIN = time_step / relax_time


def dot(a, b, ca=1, cb=0):
    return lax.dot_general(
        a,
        b,
        (((ca,), (cb,)), ((), ())),
        precision=lax.Precision.HIGHEST,
        preferred_element_type=jnp.float32,
    )


def split(x):
    high = x.astype(jnp.bfloat16)
    return high, (x - high.astype(jnp.float32)).astype(jnp.bfloat16)


def dot3(a, b, ca=1, cb=0):
    def part(x, y):
        return lax.dot_general(
            x, y, (((ca,), (cb,)), ((), ())), preferred_element_type=jnp.float32
        )

    return part(a[0], b[0]) + (part(a[0], b[1]) + part(a[1], b[0]))


def plane_scatter(parts):
    return lax.all_to_all(parts, PLANE, 0, 0, tiled=True).sum(axis=0)


def plane_gather(part):
    size = lax.axis_size(PLANE)
    parts = lax.all_to_all(
        jnp.broadcast_to(part[None], (size, *part.shape)), PLANE, 0, 0, tiled=True
    )
    return parts.reshape(size * part.shape[0], part.shape[1])


def line_total(x):
    size = lax.axis_size("zh")
    step = 1
    while step < size:
        x = x + lax.ppermute(x, "zh", [(i, i ^ step) for i in range(size)])
        step *= 2
    return x


def swap_halves(x):
    return lax.ppermute(x, "half", [(0, 1), (1, 0)])


def to_neighbour(x, distance):
    count = lax.axis_size(AXES)
    return lax.ppermute(x, CELLS, [(i, (i + distance) % count) for i in range(count)])


def whole(count):
    return [pl.BlockSpec(memory_space=pltpu.VMEM)] * count


def kernel_call(body, out, arrays, meta, scratch=()):
    outs = out if isinstance(out, list) else [out]
    results = pl.pallas_call(
        body,
        out_shape=[jax.ShapeDtypeStruct(shape, jnp.float32) for shape in outs],
        in_specs=[pl.BlockSpec(memory_space=pltpu.SMEM)] + whole(len(arrays)),
        out_specs=whole(len(outs)),
        scratch_shapes=list(scratch),
    )(meta, *arrays)
    return results if isinstance(out, list) else results[0]


B = 64


def block_inverse(d, out_ref, spread):
    rows = lax.broadcasted_iota(jnp.int32, (B, B), 0)
    cols = lax.broadcasted_iota(jnp.int32, (B, B), 1)
    eye = jnp.where(rows == cols, 1.0, 0.0).astype(jnp.float32)
    wide = jnp.concatenate([d, eye], axis=1)
    count = B // 8
    blk = [wide[8 * i : 8 * i + 8, :] for i in range(count)]
    sub = lax.broadcasted_iota(jnp.int32, (8, 2 * B), 0)

    def lane(v, j):
        return jnp.broadcast_to(v[:, j : j + 1], (8, 2 * B))

    def row(p, k, s):
        return spread[p, k, pl.ds(s, 8, stride=0), :]

    for p in range(count):
        cols_of = [[lane(blk[i], 8 * p + k) for k in range(8)] for i in range(p, count)]
        for k in range(8):
            spread[p, k, :, :] = cols_of[0][k]
        spread[p, 8, :, :] = blk[p]
        piv = {(a, b): row(p, b, a) for a in range(8) for b in range(a, 8)}
        r = [row(p, 8, a) for a in range(8)]
        done = blk[p]
        inv = {}
        for a in range(0, 8, 2):
            d00, d01, d11 = piv[a, a], piv[a, a + 1], piv[a + 1, a + 1]
            inv[a] = 1.0 / (d00 * d11 - d01 * d01)
            ratio = d01 / d00
            done = jnp.where(sub == a, r[a] * (1.0 / jnp.sqrt(d00)), done)
            last = (r[a + 1] - ratio * r[a]) * (1.0 / jnp.sqrt(d11 - ratio * d01))
            done = jnp.where(sub == a + 1, last, done)
            for b in range(a + 2, 8):
                e0, e1 = piv[a, b], piv[a + 1, b]
                t0 = (d11 * e0 - d01 * e1) * inv[a]
                t1 = (d00 * e1 - d01 * e0) * inv[a]
                for c in range(b, 8):
                    piv[b, c] = piv[b, c] - (t0 * piv[a, c] + t1 * piv[a + 1, c])
                r[b] = r[b] - (t0 * r[a] + t1 * r[a + 1])
        out_ref[8 * p : 8 * p + 8, :] = done[:, B:]
        if p + 1 < count:
            w = [None] * 8
            for a in (6, 4, 2, 0):
                y0, y1 = r[a], r[a + 1]
                for b in range(7, a + 1, -1):
                    y0 = y0 - piv[a, b] * w[b]
                    y1 = y1 - piv[a + 1, b] * w[b]
                d00, d01, d11 = piv[a, a], piv[a, a + 1], piv[a + 1, a + 1]
                w[a] = (d11 * y0 - d01 * y1) * inv[a]
                w[a + 1] = (d00 * y1 - d01 * y0) * inv[a]
            for i in range(p + 1, count):
                c = cols_of[i - p]
                even = (c[0] * w[0] + c[2] * w[2]) + (c[4] * w[4] + c[6] * w[6])
                odd = (c[1] * w[1] + c[3] * w[3]) + (c[5] * w[5] + c[7] * w[7])
                blk[i] = blk[i] - (even + odd)


def inverse_factor_body(meta, sums_ref, out_ref, work, small, spread):
    rows = lax.broadcasted_iota(jnp.int32, (R, R), 0)
    cols = lax.broadcasted_iota(jnp.int32, (R, R), 1)
    work[:H, :] = sums_ref[:H, :]
    work[H:, :H] = sums_ref[:H, H:].T
    work[H:, H:] = sums_ref[H:R, H:]
    g = work[...]
    diag = jnp.where(rows == cols, g, 0.0)
    across = 1.0 / jnp.sqrt(jnp.sum(diag, axis=0, keepdims=True))
    down = 1.0 / jnp.sqrt(jnp.sum(diag, axis=1, keepdims=True))
    work[...] = g * across * down
    for k in range(R // B):
        lo, hi = k * B, (k + 1) * B
        block_inverse(work[lo:hi, lo:hi], small, spread)
        ik = small[...]
        left = dot(ik, work[lo:hi, :])
        ccols = lax.broadcasted_iota(jnp.int32, (B, R), 1)
        wide = jnp.concatenate([ik] * (R // B), axis=1)
        panel = jnp.where((ccols >= lo) & (ccols < hi), wide, left)
        work[lo:hi, :] = panel
        if hi < R:
            at = hi // 128 * 128
            update = dot(left[:, at:], panel, 0, 0)
            below = work[hi:, :]
            bcols = lax.broadcasted_iota(jnp.int32, (R - hi, R), 1)
            below = jnp.where((bcols >= lo) & (bcols < hi), 0.0, below)
            work[hi:, :] = below - update[hi - at :, :]
    out_ref[...] = jnp.where(rows >= cols, work[...], 0.0) * across


def upper_mask():
    return lax.broadcasted_iota(jnp.int32, (R, R), 0) <= lax.broadcasted_iota(jnp.int32, (R, R), 1)


def diagonal_mask():
    return lax.broadcasted_iota(jnp.int32, (R, R), 0) == lax.broadcasted_iota(jnp.int32, (R, R), 1)


def shifted_y(x, forward):
    if forward:
        return jnp.concatenate([x[NZ:], x[:NZ]], axis=0)
    return jnp.concatenate([x[-NZ:], x[:-NZ]], axis=0)


def shifted_z(x, forward):
    count = x.shape[0]
    place = lax.broadcasted_iota(jnp.int32, x.shape, 0) & (NZ - 1)
    if forward:
        return jnp.where(
            place == NZ - 1, pltpu.roll(x, NZ - 1, 0), pltpu.roll(x, count - 1, 0)
        )
    return jnp.where(place == 0, pltpu.roll(x, count - NZ + 1, 0), pltpu.roll(x, 1, 0))


def grid_speeds(meta, count, width):
    start = meta[1]
    row = lax.broadcasted_iota(jnp.int32, (count, width), 0)
    third = (row & (NZ - 1)).astype(jnp.float32)
    second = ((start // NZ) % VGRID + row // NZ).astype(jnp.float32)
    first = (start // (NZ * VGRID)).astype(jnp.float32)
    v0 = -1.0 + (2.0 * first + 1.0) / VGRID
    v1 = -1.0 + (2.0 * second + 1.0) / VGRID
    v2 = -1.0 + (2.0 * third + 1.0) / NZ
    maxwell = jnp.exp(-2.0 * (v0 * v0 + v1 * v1 + v2 * v2))
    return v0, v1, v2, maxwell


def first_sign(meta):
    return meta[1] // (NZ * VGRID) >= VGRID // 2


def second_sign(meta):
    return (meta[1] // NZ) % VGRID >= VGRID // 2


def unpack_speed(packed, diag):
    upper, diagonal = upper_mask(), diagonal_mask()
    flipped = packed.T
    plus = jnp.where(upper, packed, flipped)
    minus = jnp.where(diagonal, diag, jnp.where(upper, flipped, packed))
    return plus, minus


def put_speed_sums(meta, f, turned, gram, scale, put_matrix, put_vector):
    upper, diagonal = upper_mask(), diagonal_mask()
    v0, v1, v2, maxwell = grid_speeds(meta, f.shape[0], R)

    def one_sign(d, value, positive):
        low = jnp.where(upper, 0.0, value)
        high = jnp.where(upper, value, 0.0)
        put_matrix(d, jnp.where(positive, high, low))
        diag = jnp.where(diagonal, value, 0.0).sum(axis=0, keepdims=True)
        put_vector(d + 1, jnp.where(positive, 0.0, diag))

    one_sign(0, v0 * gram, first_sign(meta))
    one_sign(1, dot3(turned, split(v1 * f)) * scale, second_sign(meta))
    plus = dot3(turned, split(jnp.maximum(v2, 0.0) * f)) * scale
    minus = dot3(turned, split(jnp.minimum(v2, 0.0) * f)) * scale
    put_matrix(2, jnp.where(upper, plus, minus))
    put_vector(3, jnp.where(diagonal, minus, 0.0).sum(axis=0, keepdims=True))
    put_vector(0, (f * maxwell).sum(axis=0, keepdims=True) * scale)


def first_body(total, meta, f_ref, density_ref, out_ref):
    scale = 1.0 / total
    out_ref[3 * R :, :] = jnp.zeros((R, R), jnp.float32)

    def put_vector(k, value):
        out_ref[3 * R + k : 3 * R + k + 1, :] = value

    def put_matrix(d, value):
        out_ref[d * R : (d + 1) * R, :] = value

    f = f_ref[...]
    turned = split(f.T)

    @pl.when(meta[0] == 0)
    def _():
        put_matrix(0, jnp.zeros((R, R), jnp.float32))
        put_matrix(1, dot3(turned, split(shifted_y(f, True) - f)) * scale)
        put_matrix(2, dot3(turned, split(shifted_z(f, True) - f)) * scale)
        put_vector(0, (f * density_ref[...]).sum(axis=0, keepdims=True) * scale)

    @pl.when(meta[0] == 1)
    def _():
        gram = dot3(turned, split(f)) * scale
        put_speed_sums(meta, f, turned, gram, scale, put_matrix, put_vector)


def across_body(
    place, total, meta, f_ref, previous_low_ref, previous_high_ref, sums_ref, out_ref, block, sem
):
    del sums_ref

    @pl.when(meta[0] == 0)
    def _():
        previous = jnp.concatenate([previous_low_ref[...], previous_high_ref[...]], axis=0)
        value = dot3(split(previous.T), split(f_ref[...] - previous)) * (1.0 / total)
        block[...] = value.reshape(block.shape)
        copy = pltpu.make_async_copy(block, place(out_ref), sem)
        copy.start()
        copy.wait()


def add_across(place, block, total, f, previous_low, previous_high, sums, meta):
    return pl.pallas_call(
        functools.partial(across_body, place, total),
        out_shape=jax.ShapeDtypeStruct(sums.shape, jnp.float32),
        in_specs=[pl.BlockSpec(memory_space=pltpu.SMEM)]
        + whole(3)
        + [pl.BlockSpec(memory_space=pl.ANY)],
        out_specs=pl.BlockSpec(memory_space=pl.ANY),
        scratch_shapes=[pltpu.VMEM(block, jnp.float32), pltpu.SemaphoreType.DMA(())],
        input_output_aliases={4: 0},
        name="across",
    )(meta, f, previous_low, previous_high, sums)


def next_body(
    meta,
    f_ref,
    following_ref,
    previous_low_ref,
    previous_high_ref,
    theirs_ref,
    s_ref,
    density_ref,
    low_ref,
    high_ref,
):
    half = low_ref.shape[0]

    def put(value):
        low_ref[...] = value[:half, :]
        high_ref[...] = value[half:, :]

    def vector(k):
        return theirs_ref[3 * R + k : 3 * R + k + 1, :]

    def matrix(d):
        return theirs_ref[d * R : (d + 1) * R, :]

    @pl.when(meta[0] == 0)
    def _():
        f = f_ref[...]
        following = following_ref[...]
        previous = jnp.concatenate([previous_low_ref[...], previous_high_ref[...]], axis=0)
        s = split(s_ref[...])
        out = dot3(split(f), split(KEEP * s_ref[...])) + GAIN * (density_ref[...] * vector(0))
        for d in range(3):
            plus, minus = unpack_speed(matrix(d), vector(d + 1))
            back = (previous, shifted_y(f, False), shifted_z(f, False))[d]
            ahead = (following, shifted_y(f, True), shifted_z(f, True))[d]
            change = dot3(split(f - back), split(dot3(s, split(plus))))
            change = change + dot3(split(ahead - f), split(dot3(s, split(minus))))
            out = out - time_step * change
        put(out)

    @pl.when(meta[0] == 1)
    def _():
        v0, v1, v2, maxwell = grid_speeds(meta, f_ref.shape[0], R)
        l = dot3(split(f_ref[...]), split(s_ref[...]), 1, 1)
        parts = split(l)
        out = KEEP * l + GAIN * (maxwell * vector(0))
        for d, v, positive in ((0, v0, first_sign(meta)), (1, v1, second_sign(meta))):
            e = matrix(d)
            out = out - time_step * (v * dot3(parts, split(jnp.where(positive, -e, e.T))))
        e = split(matrix(2))
        out = out + time_step * (jnp.maximum(v2, 0.0) * dot3(parts, e))
        put(out - time_step * (jnp.minimum(v2, 0.0) * dot3(parts, e, 1, 1)))


def second_body(total, meta, low_ref, high_ref, f_ref, density_ref, out_ref, k_ref, head):
    scale = 1.0 / total
    parts, rows = out_ref.shape[0], out_ref.shape[1] - 8
    per = R // rows
    k = jnp.concatenate([low_ref[...], high_ref[...]], axis=0)
    k_ref[...] = k
    straight = k.T
    gram = dot(straight, k) * scale
    turned = split(straight)
    head[:H, :] = gram[:H, :]
    head[H:, :H] = jnp.zeros((H, H), jnp.float32)
    head[H:, H:] = gram[H:, H:]

    def put_matrix(d, value):
        out_ref[per * (d + 1) : per * (d + 2), 8:, :] = value.reshape(per, rows, R)

    def put_vector(i, value):
        head[H + 2 * i : H + 2 * i + 1, :H] = value[:, :H]
        head[H + 2 * i + 1 : H + 2 * i + 2, :H] = value[:, H:]

    put_matrix(-1, dot3(turned, split(f_ref[...])) * scale)

    @pl.when(meta[0] == 0)
    def _():
        put_matrix(0, jnp.zeros((R, R), jnp.float32))
        put_matrix(1, dot3(turned, split(shifted_y(k, True) - k)) * scale)
        put_matrix(2, dot3(turned, split(shifted_z(k, True) - k)) * scale)
        put_vector(0, (k * density_ref[...]).sum(axis=0, keepdims=True) * scale)

    @pl.when(meta[0] == 1)
    def _():
        put_speed_sums(meta, k, turned, gram, scale, put_matrix, put_vector)

    out_ref[:, :8, :] = head[...].reshape(parts, 8, R)


def basis_body(meta, k_ref, inverse_ref, out_ref):
    out_ref[...] = dot(k_ref[...], inverse_ref[...].T)


def coefficient_body(
    meta,
    mine_ref,
    other_ref,
    lines_ref,
    other_lines_ref,
    inverse_ref,
    other_inverse_ref,
    s_ref,
    out_ref,
):
    def work(half, space_ref, speed_ref, space_lines, speed_lines, pk_ref, pv_ref):
        def vector(ref, k):
            return jnp.concatenate(
                [ref[2 * k : 2 * k + 1, :H], ref[2 * k + 1 : 2 * k + 2, :H]], axis=1
            )

        pk, pv = pk_ref[...], pv_ref[...]
        rows = pk[half * H : (half + 1) * H, :]
        middle = dot(dot(space_ref[:R, :], s_ref[...]), speed_ref[:R, :], 1, 1)
        turned = dot(pk, middle)
        z = dot(dot(pk, turned, 0, 0), dot(pv, pv, 0, 0))
        row_parts = split(rows)
        parts = []
        for d in range(3):
            h = split(space_ref[(1 + d) * R : (2 + d) * R, :])
            parts += [dot3(row_parts, h), dot3(row_parts, h, 1, 1)]
        parts = dot3(split(jnp.concatenate(parts, axis=0)), split(z))
        change = jnp.zeros((H, R), jnp.float32)
        for d in range(3):
            packed = speed_ref[(1 + d) * R : (2 + d) * R, :]
            plus, minus = unpack_speed(packed, vector(speed_lines, d + 1))
            change = change + dot3(split(parts[2 * d * H : (2 * d + 1) * H, :]), split(minus))
            change = change - dot3(split(parts[(2 * d + 1) * H : (2 * d + 2) * H, :]), split(plus))
        xb = jnp.sum(rows * vector(space_lines, 0), axis=1, keepdims=True)
        out = KEEP * turned[half * H : (half + 1) * H, :] - time_step * change
        out = out + GAIN * (xb * vector(speed_lines, 0))
        out_ref[...] = dot(out, pv, 1, 1)

    @pl.when(meta[0] == 0)
    def _():
        work(0, mine_ref, other_ref, lines_ref, other_lines_ref, inverse_ref, other_inverse_ref)

    @pl.when(meta[0] == 1)
    def _():
        work(1, other_ref, mine_ref, other_lines_ref, lines_ref, other_inverse_ref, inverse_ref)


def step(factors, coefficients, density):
    rows_here = factors.shape[1]
    total = rows_here * lax.axis_size(AXES)
    start = lax.axis_index(AXES) * rows_here
    meta = jnp.stack([lax.axis_index("half"), start]).astype(jnp.int32)
    f = factors[0]
    column = density[:, None]

    half = rows_here // 2
    low, high = f[:half], f[half:]
    previous_high = to_neighbour(high, 1)
    previous_low = to_neighbour(low, 1)
    following = to_neighbour(f, -1)

    sums = kernel_call(functools.partial(first_body, total), (4 * R, R), [f, column], meta)
    sums = add_across(
        lambda ref: ref.at[pl.ds(0, R), :], (R, R), total, f, previous_low, previous_high, sums, meta
    )
    theirs = plane_gather(
        swap_halves(line_total(plane_scatter(sums.reshape(lax.axis_size(PLANE), -1, R))))
    )
    low, high = kernel_call(
        next_body,
        [(half, R)] * 2,
        [f, following, previous_low, previous_high, theirs, coefficients, column],
        meta,
    )

    before_high = to_neighbour(high, 1)
    before_low = to_neighbour(low, 1)
    parts = lax.axis_size(PLANE)
    rows = 4 * R // parts
    per = R // rows
    sums, fresh = kernel_call(
        functools.partial(second_body, total),
        [(parts, 8 + rows, R), (rows_here, R)],
        [low, high, f, column],
        meta,
        [pltpu.VMEM((R, R), jnp.float32)],
    )
    sums = add_across(
        lambda ref: ref.at[pl.ds(per, per), pl.ds(8, rows), :],
        (per, rows, R),
        total,
        fresh,
        before_low,
        before_high,
        sums,
        meta,
    )
    part = line_total(plane_scatter(sums))
    head = plane_gather(part[:8])
    head, rest = lax.optimization_barrier((head, part[8:]))
    mine = plane_gather(rest)
    lines = head[H : H + 16]
    other_lines = swap_halves(lines)
    inverse = kernel_call(
        inverse_factor_body,
        (R, R),
        [head],
        meta,
        [
            pltpu.VMEM((R, R), jnp.float32),
            pltpu.VMEM((B, B), jnp.float32),
            pltpu.VMEM((B // 8, 9, 8, 2 * B), jnp.float32),
        ],
    )
    basis = kernel_call(basis_body, (rows_here, R), [fresh, inverse], meta)
    other_inverse = swap_halves(inverse)
    other = swap_halves(mine)
    updated = kernel_call(
        coefficient_body,
        (H, R),
        [mine, other, lines, other_lines, inverse, other_inverse, coefficients],
        meta,
    )
    return (basis[None], updated)


def solution(mesh):
    torus = Mesh(mesh.devices.reshape(mesh.shape["half"], 4, 4, 4, 2), CELLS)
    return jax.shard_map(
        step,
        mesh=torus,
        in_specs=(P("half", AXES, None), P(), P(AXES)),
        out_specs=(P("half", AXES, None), P("half", None)),
        check_vma=False,
    )
```

```python
import functools

import jax
import jax.numpy as jnp
from jax import lax
from jax.experimental import pallas as pl
from jax.experimental.pallas import tpu as pltpu
from jax.sharding import Mesh
from jax.sharding import PartitionSpec as P

NZ = 32
VGRID = 64
R = 256
H = R // 2
AXES = ("y", "x", "zh", "zl")
PLANE = ("y", "x", "zl")
CELLS = ("half", "y", "x", "zh", "zl")

time_step = 0.2
relax_time = 0.5
KEEP = 1.0 - time_step / relax_time
GAIN = time_step / relax_time


def dot(a, b, ca=1, cb=0):
    return lax.dot_general(
        a,
        b,
        (((ca,), (cb,)), ((), ())),
        precision=lax.Precision.HIGHEST,
        preferred_element_type=jnp.float32,
    )


def split(x):
    high = x.astype(jnp.bfloat16)
    return high, (x - high.astype(jnp.float32)).astype(jnp.bfloat16)


def dot3(a, b, ca=1, cb=0):
    def part(x, y):
        return lax.dot_general(
            x, y, (((ca,), (cb,)), ((), ())), preferred_element_type=jnp.float32
        )

    return part(a[0], b[0]) + (part(a[0], b[1]) + part(a[1], b[0]))


def plane_scatter(x):
    parts = x.reshape(lax.axis_size(PLANE), -1, x.shape[1])
    return lax.all_to_all(parts, PLANE, 0, 0, tiled=True).sum(axis=0)


def plane_gather(part):
    size = lax.axis_size(PLANE)
    parts = lax.all_to_all(
        jnp.broadcast_to(part[None], (size, *part.shape)), PLANE, 0, 0, tiled=True
    )
    return parts.reshape(size * part.shape[0], part.shape[1])


def line_total(x):
    size = lax.axis_size("zh")
    step = 1
    while step < size:
        x = x + lax.ppermute(x, "zh", [(i, i ^ step) for i in range(size)])
        step *= 2
    return x


def swap_halves(x):
    return lax.ppermute(x, "half", [(0, 1), (1, 0)])


def to_neighbour(x, distance):
    count = lax.axis_size(AXES)
    return lax.ppermute(x, CELLS, [(i, (i + distance) % count) for i in range(count)])


def whole(count):
    return [pl.BlockSpec(memory_space=pltpu.VMEM)] * count


def kernel_call(body, out, arrays, meta, scratch=()):
    outs = out if isinstance(out, list) else [out]
    results = pl.pallas_call(
        body,
        out_shape=[jax.ShapeDtypeStruct(shape, jnp.float32) for shape in outs],
        in_specs=[pl.BlockSpec(memory_space=pltpu.SMEM)] + whole(len(arrays)),
        out_specs=whole(len(outs)),
        scratch_shapes=list(scratch),
    )(meta, *arrays)
    return results if isinstance(out, list) else results[0]


B = 64


def block_inverse(d, out_ref, spread):
    rows = lax.broadcasted_iota(jnp.int32, (B, B), 0)
    cols = lax.broadcasted_iota(jnp.int32, (B, B), 1)
    eye = jnp.where(rows == cols, 1.0, 0.0).astype(jnp.float32)
    wide = jnp.concatenate([d, eye], axis=1)
    count = B // 8
    blk = [wide[8 * i : 8 * i + 8, :] for i in range(count)]
    sub = lax.broadcasted_iota(jnp.int32, (8, 2 * B), 0)

    def lane(v, j):
        return jnp.broadcast_to(v[:, j : j + 1], (8, 2 * B))

    def row(p, k, s):
        return spread[p, k, pl.ds(s, 8, stride=0), :]

    for p in range(count):
        cols_of = [[lane(blk[i], 8 * p + k) for k in range(8)] for i in range(p, count)]
        for k in range(8):
            spread[p, k, :, :] = cols_of[0][k]
        spread[p, 8, :, :] = blk[p]
        piv = {(a, b): row(p, b, a) for a in range(8) for b in range(a, 8)}
        r = [row(p, 8, a) for a in range(8)]
        done = blk[p]
        inv = {}
        for a in range(0, 8, 2):
            d00, d01, d11 = piv[a, a], piv[a, a + 1], piv[a + 1, a + 1]
            inv[a] = 1.0 / (d00 * d11 - d01 * d01)
            ratio = d01 / d00
            done = jnp.where(sub == a, r[a] * (1.0 / jnp.sqrt(d00)), done)
            last = (r[a + 1] - ratio * r[a]) * (1.0 / jnp.sqrt(d11 - ratio * d01))
            done = jnp.where(sub == a + 1, last, done)
            for b in range(a + 2, 8):
                e0, e1 = piv[a, b], piv[a + 1, b]
                t0 = (d11 * e0 - d01 * e1) * inv[a]
                t1 = (d00 * e1 - d01 * e0) * inv[a]
                for c in range(b, 8):
                    piv[b, c] = piv[b, c] - (t0 * piv[a, c] + t1 * piv[a + 1, c])
                r[b] = r[b] - (t0 * r[a] + t1 * r[a + 1])
        out_ref[8 * p : 8 * p + 8, :] = done[:, B:]
        if p + 1 < count:
            w = [None] * 8
            for a in (6, 4, 2, 0):
                y0, y1 = r[a], r[a + 1]
                for b in range(7, a + 1, -1):
                    y0 = y0 - piv[a, b] * w[b]
                    y1 = y1 - piv[a + 1, b] * w[b]
                d00, d01, d11 = piv[a, a], piv[a, a + 1], piv[a + 1, a + 1]
                w[a] = (d11 * y0 - d01 * y1) * inv[a]
                w[a + 1] = (d00 * y1 - d01 * y0) * inv[a]
            for i in range(p + 1, count):
                c = cols_of[i - p]
                even = (c[0] * w[0] + c[2] * w[2]) + (c[4] * w[4] + c[6] * w[6])
                odd = (c[1] * w[1] + c[3] * w[3]) + (c[5] * w[5] + c[7] * w[7])
                blk[i] = blk[i] - (even + odd)


def inverse_factor_body(meta, sums_ref, out_ref, work, small, spread):
    rows = lax.broadcasted_iota(jnp.int32, (R, R), 0)
    cols = lax.broadcasted_iota(jnp.int32, (R, R), 1)
    work[:H, :] = sums_ref[:H, :]
    work[H:, :H] = sums_ref[:H, H:].T
    work[H:, H:] = sums_ref[H:R, H:]
    g = work[...]
    diag = jnp.where(rows == cols, g, 0.0)
    across = 1.0 / jnp.sqrt(jnp.sum(diag, axis=0, keepdims=True))
    down = 1.0 / jnp.sqrt(jnp.sum(diag, axis=1, keepdims=True))
    work[...] = g * across * down
    for k in range(R // B):
        lo, hi = k * B, (k + 1) * B
        block_inverse(work[lo:hi, lo:hi], small, spread)
        ik = small[...]
        left = dot(ik, work[lo:hi, :])
        ccols = lax.broadcasted_iota(jnp.int32, (B, R), 1)
        wide = jnp.concatenate([ik] * (R // B), axis=1)
        panel = jnp.where((ccols >= lo) & (ccols < hi), wide, left)
        work[lo:hi, :] = panel
        if hi < R:
            at = hi // 128 * 128
            update = dot(left[:, at:], panel, 0, 0)
            below = work[hi:, :]
            bcols = lax.broadcasted_iota(jnp.int32, (R - hi, R), 1)
            below = jnp.where((bcols >= lo) & (bcols < hi), 0.0, below)
            work[hi:, :] = below - update[hi - at :, :]
    out_ref[...] = jnp.where(rows >= cols, work[...], 0.0) * across


def upper_mask():
    return lax.broadcasted_iota(jnp.int32, (R, R), 0) <= lax.broadcasted_iota(jnp.int32, (R, R), 1)


def diagonal_mask():
    return lax.broadcasted_iota(jnp.int32, (R, R), 0) == lax.broadcasted_iota(jnp.int32, (R, R), 1)


def shifted_y(x, forward):
    if forward:
        return jnp.concatenate([x[NZ:], x[:NZ]], axis=0)
    return jnp.concatenate([x[-NZ:], x[:-NZ]], axis=0)


def shifted_z(x, forward):
    count = x.shape[0]
    place = lax.broadcasted_iota(jnp.int32, x.shape, 0) & (NZ - 1)
    if forward:
        return jnp.where(
            place == NZ - 1, pltpu.roll(x, NZ - 1, 0), pltpu.roll(x, count - 1, 0)
        )
    return jnp.where(place == 0, pltpu.roll(x, count - NZ + 1, 0), pltpu.roll(x, 1, 0))


def grid_speeds(meta, count, width):
    start = meta[1]
    row = lax.broadcasted_iota(jnp.int32, (count, width), 0)
    third = (row & (NZ - 1)).astype(jnp.float32)
    second = ((start // NZ) % VGRID + row // NZ).astype(jnp.float32)
    first = (start // (NZ * VGRID)).astype(jnp.float32)
    v0 = -1.0 + (2.0 * first + 1.0) / VGRID
    v1 = -1.0 + (2.0 * second + 1.0) / VGRID
    v2 = -1.0 + (2.0 * third + 1.0) / NZ
    maxwell = jnp.exp(-2.0 * (v0 * v0 + v1 * v1 + v2 * v2))
    return v0, v1, v2, maxwell


def first_sign(meta):
    return meta[1] // (NZ * VGRID) >= VGRID // 2


def second_sign(meta):
    return (meta[1] // NZ) % VGRID >= VGRID // 2


def unpack_speed(packed, diag):
    upper, diagonal = upper_mask(), diagonal_mask()
    flipped = packed.T
    plus = jnp.where(upper, packed, flipped)
    minus = jnp.where(diagonal, diag, jnp.where(upper, flipped, packed))
    return plus, minus


def put_speed_sums(meta, f, turned, gram, scale, put_matrix, put_vector):
    upper, diagonal = upper_mask(), diagonal_mask()
    v0, v1, v2, maxwell = grid_speeds(meta, f.shape[0], R)

    def one_sign(d, value, positive):
        low = jnp.where(upper, 0.0, value)
        high = jnp.where(upper, value, 0.0)
        put_matrix(d, jnp.where(positive, high, low))
        diag = jnp.where(diagonal, value, 0.0).sum(axis=0, keepdims=True)
        put_vector(d + 1, jnp.where(positive, 0.0, diag))

    one_sign(0, v0 * gram, first_sign(meta))
    one_sign(1, dot3(turned, split(v1 * f)) * scale, second_sign(meta))
    plus = dot3(turned, split(jnp.maximum(v2, 0.0) * f)) * scale
    minus = dot3(turned, split(jnp.minimum(v2, 0.0) * f)) * scale
    put_matrix(2, jnp.where(upper, plus, minus))
    put_vector(3, jnp.where(diagonal, minus, 0.0).sum(axis=0, keepdims=True))
    put_vector(0, (f * maxwell).sum(axis=0, keepdims=True) * scale)


def first_body(total, meta, f_ref, density_ref, out_ref):
    scale = 1.0 / total
    out_ref[3 * R :, :] = jnp.zeros((R, R), jnp.float32)

    def put_vector(k, value):
        out_ref[3 * R + k : 3 * R + k + 1, :] = value

    def put_matrix(d, value):
        out_ref[d * R : (d + 1) * R, :] = value

    f = f_ref[...]
    turned = split(f.T)

    @pl.when(meta[0] == 0)
    def _():
        put_matrix(0, jnp.zeros((R, R), jnp.float32))
        put_matrix(1, dot3(turned, split(shifted_y(f, True) - f)) * scale)
        put_matrix(2, dot3(turned, split(shifted_z(f, True) - f)) * scale)
        put_vector(0, (f * density_ref[...]).sum(axis=0, keepdims=True) * scale)

    @pl.when(meta[0] == 1)
    def _():
        gram = dot3(turned, split(f)) * scale
        put_speed_sums(meta, f, turned, gram, scale, put_matrix, put_vector)


def across_body(at, total, pairs, meta, *refs):
    *planes, sums_ref, out_ref, block, sem = refs
    del sums_ref

    @pl.when(meta[0] == 0)
    def _():
        left, right = pairs(*planes)
        block[...] = dot3(split(left.T), split(right - left)) * (1.0 / total)
        copy = pltpu.make_async_copy(block, out_ref.at[pl.ds(at, R), :], sem)
        copy.start()
        copy.wait()


def add_across(at, total, pairs, planes, sums, meta):
    return pl.pallas_call(
        functools.partial(across_body, at, total, pairs),
        out_shape=jax.ShapeDtypeStruct(sums.shape, jnp.float32),
        in_specs=[pl.BlockSpec(memory_space=pltpu.SMEM)]
        + whole(len(planes))
        + [pl.BlockSpec(memory_space=pl.ANY)],
        out_specs=pl.BlockSpec(memory_space=pl.ANY),
        scratch_shapes=[pltpu.VMEM((R, R), jnp.float32), pltpu.SemaphoreType.DMA(())],
        input_output_aliases={len(planes) + 1: 0},
        name="across",
    )(meta, *planes, sums)


def with_plane_before(f_ref, previous_low_ref, previous_high_ref):
    return jnp.concatenate([previous_low_ref[...], previous_high_ref[...]], axis=0), f_ref[...]


def with_half_planes(low_ref, high_ref, after_low_ref, before_high_ref):
    left = jnp.concatenate([low_ref[...], before_high_ref[...]], axis=0)
    return left, jnp.concatenate([after_low_ref[...], high_ref[...]], axis=0)


def next_body(
    meta,
    f_ref,
    following_ref,
    previous_low_ref,
    previous_high_ref,
    theirs_ref,
    s_ref,
    density_ref,
    low_ref,
    high_ref,
):
    half = low_ref.shape[0]

    def put(value):
        low_ref[...] = value[:half, :]
        high_ref[...] = value[half:, :]

    def vector(k):
        return theirs_ref[3 * R + k : 3 * R + k + 1, :]

    def matrix(d):
        return theirs_ref[d * R : (d + 1) * R, :]

    @pl.when(meta[0] == 0)
    def _():
        f = f_ref[...]
        following = following_ref[...]
        previous = jnp.concatenate([previous_low_ref[...], previous_high_ref[...]], axis=0)
        s = split(s_ref[...])
        out = dot3(split(f), split(KEEP * s_ref[...])) + GAIN * (density_ref[...] * vector(0))
        for d in range(3):
            plus, minus = unpack_speed(matrix(d), vector(d + 1))
            back = (previous, shifted_y(f, False), shifted_z(f, False))[d]
            ahead = (following, shifted_y(f, True), shifted_z(f, True))[d]
            change = dot3(split(f - back), split(dot3(s, split(plus))))
            change = change + dot3(split(ahead - f), split(dot3(s, split(minus))))
            out = out - time_step * change
        put(out)

    @pl.when(meta[0] == 1)
    def _():
        v0, v1, v2, maxwell = grid_speeds(meta, f_ref.shape[0], R)
        l = dot3(split(f_ref[...]), split(s_ref[...]), 1, 1)
        parts = split(l)
        out = KEEP * l + GAIN * (maxwell * vector(0))
        for d, v, positive in ((0, v0, first_sign(meta)), (1, v1, second_sign(meta))):
            e = matrix(d)
            out = out - time_step * (v * dot3(parts, split(jnp.where(positive, -e, e.T))))
        e = split(matrix(2))
        out = out + time_step * (jnp.maximum(v2, 0.0) * dot3(parts, e))
        put(out - time_step * (jnp.minimum(v2, 0.0) * dot3(parts, e, 1, 1)))


def second_body(total, meta, low_ref, high_ref, f_ref, density_ref, out_ref, k_ref):
    scale = 1.0 / total
    k = jnp.concatenate([low_ref[...], high_ref[...]], axis=0)
    k_ref[...] = k
    straight = k.T
    gram = dot(straight, k) * scale
    turned = split(straight)
    out_ref[:H, :] = gram[:H, :]
    out_ref[H:R, :H] = jnp.zeros((H, H), jnp.float32)
    out_ref[H:R, H:] = gram[H:, H:]

    def put_matrix(d, value):
        out_ref[(2 + d) * R : (3 + d) * R, :] = value

    def put_vector(i, value):
        out_ref[H + 2 * i : H + 2 * i + 1, :H] = value[:, :H]
        out_ref[H + 2 * i + 1 : H + 2 * i + 2, :H] = value[:, H:]

    put_matrix(-1, dot3(turned, split(f_ref[...])) * scale)

    @pl.when(meta[0] == 0)
    def _():
        put_matrix(0, jnp.zeros((R, R), jnp.float32))
        put_matrix(1, dot3(turned, split(shifted_y(k, True) - k)) * scale)
        put_matrix(2, dot3(turned, split(shifted_z(k, True) - k)) * scale)
        put_vector(0, (k * density_ref[...]).sum(axis=0, keepdims=True) * scale)

    @pl.when(meta[0] == 1)
    def _():
        put_speed_sums(meta, k, turned, gram, scale, put_matrix, put_vector)


def basis_body(meta, k_ref, inverse_ref, out_ref):
    out_ref[...] = dot(k_ref[...], inverse_ref[...].T)


def coefficient_body(
    meta,
    mine_ref,
    other_ref,
    inverse_ref,
    other_inverse_ref,
    s_ref,
    out_ref,
):
    def work(half, space_ref, speed_ref, pk_ref, pv_ref):
        def vector(ref, k):
            at = H + 2 * k
            return jnp.concatenate([ref[at : at + 1, :H], ref[at + 1 : at + 2, :H]], axis=1)

        pk, pv = pk_ref[...], pv_ref[...]
        rows = pk[half * H : (half + 1) * H, :]
        middle = dot(dot(space_ref[R : 2 * R, :], s_ref[...]), speed_ref[R : 2 * R, :], 1, 1)
        turned = dot(pk, middle)
        z = dot(dot(pk, turned, 0, 0), dot(pv, pv, 0, 0))
        row_parts = split(rows)
        parts = []
        for d in range(3):
            h = split(space_ref[(2 + d) * R : (3 + d) * R, :])
            parts += [dot3(row_parts, h), dot3(row_parts, h, 1, 1)]
        parts = dot3(split(jnp.concatenate(parts, axis=0)), split(z))
        change = jnp.zeros((H, R), jnp.float32)
        for d in range(3):
            packed = speed_ref[(2 + d) * R : (3 + d) * R, :]
            plus, minus = unpack_speed(packed, vector(speed_ref, d + 1))
            change = change + dot3(split(parts[2 * d * H : (2 * d + 1) * H, :]), split(minus))
            change = change - dot3(split(parts[(2 * d + 1) * H : (2 * d + 2) * H, :]), split(plus))
        xb = jnp.sum(rows * vector(space_ref, 0), axis=1, keepdims=True)
        out = KEEP * turned[half * H : (half + 1) * H, :] - time_step * change
        out = out + GAIN * (xb * vector(speed_ref, 0))
        out_ref[...] = dot(out, pv, 1, 1)

    @pl.when(meta[0] == 0)
    def _():
        work(0, mine_ref, other_ref, inverse_ref, other_inverse_ref)

    @pl.when(meta[0] == 1)
    def _():
        work(1, other_ref, mine_ref, other_inverse_ref, inverse_ref)


def step(factors, coefficients, density):
    rows_here = factors.shape[1]
    total = rows_here * lax.axis_size(AXES)
    start = lax.axis_index(AXES) * rows_here
    meta = jnp.stack([lax.axis_index("half"), start]).astype(jnp.int32)
    f = factors[0]
    column = density[:, None]

    half = rows_here // 2
    low, high = f[:half], f[half:]
    previous_high = to_neighbour(high, 1)
    previous_low = to_neighbour(low, 1)
    following = to_neighbour(f, -1)

    sums = kernel_call(functools.partial(first_body, total), (4 * R, R), [f, column], meta)
    sums = add_across(0, total, with_plane_before, [f, previous_low, previous_high], sums, meta)
    theirs = plane_gather(swap_halves(line_total(plane_scatter(sums))))
    low, high = kernel_call(
        next_body,
        [(half, R)] * 2,
        [f, following, previous_low, previous_high, theirs, coefficients, column],
        meta,
    )

    before_high = to_neighbour(high, 1)
    after_low = to_neighbour(low, -1)
    sums, fresh = kernel_call(
        functools.partial(second_body, total),
        [(5 * R, R), (rows_here, R)],
        [low, high, f, column],
        meta,
    )
    sums = add_across(
        2 * R, total, with_half_planes, [low, high, after_low, before_high], sums, meta
    )
    mine = plane_gather(line_total(plane_scatter(sums)))
    other = swap_halves(mine)
    inverse = kernel_call(
        inverse_factor_body,
        (R, R),
        [mine],
        meta,
        [
            pltpu.VMEM((R, R), jnp.float32),
            pltpu.VMEM((B, B), jnp.float32),
            pltpu.VMEM((B // 8, 9, 8, 2 * B), jnp.float32),
        ],
    )
    basis = kernel_call(basis_body, (rows_here, R), [fresh, inverse], meta)
    other_inverse = swap_halves(inverse)
    updated = kernel_call(
        coefficient_body, (H, R), [mine, other, inverse, other_inverse, coefficients], meta
    )
    return (basis[None], updated)


def solution(mesh):
    torus = Mesh(mesh.devices.reshape(mesh.shape["half"], 4, 4, 4, 2), CELLS)
    return jax.shard_map(
        step,
        mesh=torus,
        in_specs=(P("half", AXES, None), P(), P(AXES)),
        out_specs=(P("half", AXES, None), P("half", None)),
        check_vma=False,
    )
```

```python
import functools

import jax
import jax.numpy as jnp
from jax import lax
from jax.experimental import pallas as pl
from jax.experimental.pallas import tpu as pltpu
from jax.sharding import Mesh
from jax.sharding import PartitionSpec as P

NZ = 32
VGRID = 64
R = 256
H = R // 2
VMEM_LIMIT = 20 << 20
AXES = ("y", "x", "zh", "zl")
PLANE = ("y", "x", "zl")
CELLS = ("half", "y", "x", "zh", "zl")

time_step = 0.2
relax_time = 0.5
KEEP = 1.0 - time_step / relax_time
GAIN = time_step / relax_time


def dot(a, b, ca=1, cb=0):
    return lax.dot_general(
        a,
        b,
        (((ca,), (cb,)), ((), ())),
        precision=lax.Precision.HIGHEST,
        preferred_element_type=jnp.float32,
    )


def split(x):
    high = x.astype(jnp.bfloat16)
    return high, (x - high.astype(jnp.float32)).astype(jnp.bfloat16)


def dot3(a, b, ca=1, cb=0):
    def part(x, y):
        return lax.dot_general(
            x, y, (((ca,), (cb,)), ((), ())), preferred_element_type=jnp.float32
        )

    return part(a[0], b[0]) + (part(a[0], b[1]) + part(a[1], b[0]))


def plane_scatter(x):
    parts = x.reshape(lax.axis_size(PLANE), -1, x.shape[1])
    return lax.all_to_all(parts, PLANE, 0, 0, tiled=True).sum(axis=0)


def plane_gather(part):
    size = lax.axis_size(PLANE)
    parts = lax.all_to_all(
        jnp.broadcast_to(part[None], (size, *part.shape)), PLANE, 0, 0, tiled=True
    )
    return parts.reshape(size * part.shape[0], part.shape[1])


def line_total(x):
    size = lax.axis_size("zh")
    step = 1
    while step < size:
        x = x + lax.ppermute(x, "zh", [(i, i ^ step) for i in range(size)])
        step *= 2
    return x


def swap_halves(x):
    return lax.ppermute(x, "half", [(0, 1), (1, 0)])


def to_neighbour(x, distance):
    count = lax.axis_size(AXES)
    return lax.ppermute(x, CELLS, [(i, (i + distance) % count) for i in range(count)])


def whole(count):
    return [pl.BlockSpec(memory_space=pltpu.VMEM)] * count


def kernel_call(body, out, arrays, meta, scratch=(), fetch=False):
    outs = out if isinstance(out, list) else [out]
    results = pl.pallas_call(
        body,
        out_shape=[jax.ShapeDtypeStruct(shape, jnp.float32) for shape in outs],
        in_specs=[pl.BlockSpec(memory_space=pltpu.SMEM)]
        + ([pl.BlockSpec(memory_space=pl.ANY)] * len(arrays) if fetch else whole(len(arrays))),
        out_specs=whole(len(outs)),
        scratch_shapes=list(scratch),
        compiler_params=pltpu.CompilerParams(vmem_limit_bytes=VMEM_LIMIT),
    )(meta, *arrays)
    return results if isinstance(out, list) else results[0]


B = 64


def block_inverse(d, out_ref, spread):
    rows = lax.broadcasted_iota(jnp.int32, (B, B), 0)
    cols = lax.broadcasted_iota(jnp.int32, (B, B), 1)
    eye = jnp.where(rows == cols, 1.0, 0.0).astype(jnp.float32)
    wide = jnp.concatenate([d, eye], axis=1)
    count = B // 8
    blk = [wide[8 * i : 8 * i + 8, :] for i in range(count)]
    sub = lax.broadcasted_iota(jnp.int32, (8, 2 * B), 0)

    def lane(v, j):
        return jnp.broadcast_to(v[:, j : j + 1], (8, 2 * B))

    def row(p, k, s):
        return spread[p, k, pl.ds(s, 8, stride=0), :]

    for p in range(count):
        cols_of = [[lane(blk[i], 8 * p + k) for k in range(8)] for i in range(p, count)]
        for k in range(8):
            spread[p, k, :, :] = cols_of[0][k]
        spread[p, 8, :, :] = blk[p]
        piv = {(a, b): row(p, b, a) for a in range(8) for b in range(a, 8)}
        r = [row(p, 8, a) for a in range(8)]
        done = blk[p]
        inv = {}
        for a in range(0, 8, 2):
            d00, d01, d11 = piv[a, a], piv[a, a + 1], piv[a + 1, a + 1]
            inv[a] = 1.0 / (d00 * d11 - d01 * d01)
            ratio = d01 / d00
            done = jnp.where(sub == a, r[a] * (1.0 / jnp.sqrt(d00)), done)
            last = (r[a + 1] - ratio * r[a]) * (1.0 / jnp.sqrt(d11 - ratio * d01))
            done = jnp.where(sub == a + 1, last, done)
            for b in range(a + 2, 8):
                e0, e1 = piv[a, b], piv[a + 1, b]
                t0 = (d11 * e0 - d01 * e1) * inv[a]
                t1 = (d00 * e1 - d01 * e0) * inv[a]
                for c in range(b, 8):
                    piv[b, c] = piv[b, c] - (t0 * piv[a, c] + t1 * piv[a + 1, c])
                r[b] = r[b] - (t0 * r[a] + t1 * r[a + 1])
        out_ref[8 * p : 8 * p + 8, :] = done[:, B:]
        if p + 1 < count:
            w = [None] * 8
            for a in (6, 4, 2, 0):
                y0, y1 = r[a], r[a + 1]
                for b in range(7, a + 1, -1):
                    y0 = y0 - piv[a, b] * w[b]
                    y1 = y1 - piv[a + 1, b] * w[b]
                d00, d01, d11 = piv[a, a], piv[a, a + 1], piv[a + 1, a + 1]
                w[a] = (d11 * y0 - d01 * y1) * inv[a]
                w[a + 1] = (d00 * y1 - d01 * y0) * inv[a]
            for i in range(p + 1, count):
                c = cols_of[i - p]
                even = (c[0] * w[0] + c[2] * w[2]) + (c[4] * w[4] + c[6] * w[6])
                odd = (c[1] * w[1] + c[3] * w[3]) + (c[5] * w[5] + c[7] * w[7])
                blk[i] = blk[i] - (even + odd)


def inverse_factor_body(meta, sums_ref, out_ref, work, small, spread, gram_ref, sem):
    copy = pltpu.make_async_copy(sums_ref.at[pl.ds(0, R), :], gram_ref, sem)
    copy.start()
    copy.wait()
    rows = lax.broadcasted_iota(jnp.int32, (R, R), 0)
    cols = lax.broadcasted_iota(jnp.int32, (R, R), 1)
    work[:H, :] = gram_ref[:H, :]
    work[H:, :H] = gram_ref[:H, H:].T
    work[H:, H:] = gram_ref[H:R, H:]
    g = work[...]
    diag = jnp.where(rows == cols, g, 0.0)
    across = 1.0 / jnp.sqrt(jnp.sum(diag, axis=0, keepdims=True))
    down = 1.0 / jnp.sqrt(jnp.sum(diag, axis=1, keepdims=True))
    work[...] = g * across * down
    for k in range(R // B):
        lo, hi = k * B, (k + 1) * B
        block_inverse(work[lo:hi, lo:hi], small, spread)
        ik = small[...]
        left = dot(ik, work[lo:hi, :])
        ccols = lax.broadcasted_iota(jnp.int32, (B, R), 1)
        wide = jnp.concatenate([ik] * (R // B), axis=1)
        panel = jnp.where((ccols >= lo) & (ccols < hi), wide, left)
        work[lo:hi, :] = panel
        if hi < R:
            at = hi // 128 * 128
            update = dot(left[:, at:], panel, 0, 0)
            below = work[hi:, :]
            bcols = lax.broadcasted_iota(jnp.int32, (R - hi, R), 1)
            below = jnp.where((bcols >= lo) & (bcols < hi), 0.0, below)
            work[hi:, :] = below - update[hi - at :, :]
    out_ref[...] = jnp.where(rows >= cols, work[...], 0.0) * across


def upper_mask():
    return lax.broadcasted_iota(jnp.int32, (R, R), 0) <= lax.broadcasted_iota(jnp.int32, (R, R), 1)


def diagonal_mask():
    return lax.broadcasted_iota(jnp.int32, (R, R), 0) == lax.broadcasted_iota(jnp.int32, (R, R), 1)


def shifted_y(x, forward):
    if forward:
        return jnp.concatenate([x[NZ:], x[:NZ]], axis=0)
    return jnp.concatenate([x[-NZ:], x[:-NZ]], axis=0)


def shifted_z(x, forward):
    count = x.shape[0]
    place = lax.broadcasted_iota(jnp.int32, x.shape, 0) & (NZ - 1)
    if forward:
        return jnp.where(
            place == NZ - 1, pltpu.roll(x, NZ - 1, 0), pltpu.roll(x, count - 1, 0)
        )
    return jnp.where(place == 0, pltpu.roll(x, count - NZ + 1, 0), pltpu.roll(x, 1, 0))


def grid_speeds(meta, count, width):
    start = meta[1]
    row = lax.broadcasted_iota(jnp.int32, (count, width), 0)
    third = (row & (NZ - 1)).astype(jnp.float32)
    second = ((start // NZ) % VGRID + row // NZ).astype(jnp.float32)
    first = (start // (NZ * VGRID)).astype(jnp.float32)
    v0 = -1.0 + (2.0 * first + 1.0) / VGRID
    v1 = -1.0 + (2.0 * second + 1.0) / VGRID
    v2 = -1.0 + (2.0 * third + 1.0) / NZ
    maxwell = jnp.exp(-2.0 * (v0 * v0 + v1 * v1 + v2 * v2))
    return v0, v1, v2, maxwell


def first_sign(meta):
    return meta[1] // (NZ * VGRID) >= VGRID // 2


def second_sign(meta):
    return (meta[1] // NZ) % VGRID >= VGRID // 2


def unpack_speed(packed, diag):
    upper, diagonal = upper_mask(), diagonal_mask()
    flipped = packed.T
    plus = jnp.where(upper, packed, flipped)
    minus = jnp.where(diagonal, diag, jnp.where(upper, flipped, packed))
    return plus, minus


def put_speed_sums(meta, f, turned, gram, scale, put_matrix, put_vector):
    upper, diagonal = upper_mask(), diagonal_mask()
    v0, v1, v2, maxwell = grid_speeds(meta, f.shape[0], R)

    def one_sign(d, value, positive):
        low = jnp.where(upper, 0.0, value)
        high = jnp.where(upper, value, 0.0)
        put_matrix(d, jnp.where(positive, high, low))
        diag = jnp.where(diagonal, value, 0.0).sum(axis=0, keepdims=True)
        put_vector(d + 1, jnp.where(positive, 0.0, diag))

    one_sign(0, v0 * gram, first_sign(meta))
    one_sign(1, dot3(turned, split(v1 * f)) * scale, second_sign(meta))
    plus = dot3(turned, split(jnp.maximum(v2, 0.0) * f)) * scale
    minus = dot3(turned, split(jnp.minimum(v2, 0.0) * f)) * scale
    put_matrix(2, jnp.where(upper, plus, minus))
    put_vector(3, jnp.where(diagonal, minus, 0.0).sum(axis=0, keepdims=True))
    put_vector(0, (f * maxwell).sum(axis=0, keepdims=True) * scale)


def first_body(total, meta, f_ref, density_ref, out_ref):
    scale = 1.0 / total
    out_ref[3 * R :, :] = jnp.zeros((R, R), jnp.float32)

    def put_vector(k, value):
        out_ref[3 * R + k : 3 * R + k + 1, :] = value

    def put_matrix(d, value):
        out_ref[d * R : (d + 1) * R, :] = value

    f = f_ref[...]
    turned = split(f.T)

    @pl.when(meta[0] == 0)
    def _():
        put_matrix(0, jnp.zeros((R, R), jnp.float32))
        put_matrix(1, dot3(turned, split(shifted_y(f, True) - f)) * scale)
        put_matrix(2, dot3(turned, split(shifted_z(f, True) - f)) * scale)
        put_vector(0, (f * density_ref[...]).sum(axis=0, keepdims=True) * scale)

    @pl.when(meta[0] == 1)
    def _():
        gram = dot3(turned, split(f)) * scale
        put_speed_sums(meta, f, turned, gram, scale, put_matrix, put_vector)


def across_body(at, total, pairs, meta, *refs):
    *planes, sums_ref, out_ref, block, sem = refs
    del sums_ref

    @pl.when(meta[0] == 0)
    def _():
        left, right = pairs(*planes)
        block[...] = dot3(split(left.T), split(right - left)) * (1.0 / total)
        copy = pltpu.make_async_copy(block, out_ref.at[pl.ds(at, R), :], sem)
        copy.start()
        copy.wait()


def add_across(at, total, pairs, planes, sums, meta):
    return pl.pallas_call(
        functools.partial(across_body, at, total, pairs),
        out_shape=jax.ShapeDtypeStruct(sums.shape, jnp.float32),
        in_specs=[pl.BlockSpec(memory_space=pltpu.SMEM)]
        + whole(len(planes))
        + [pl.BlockSpec(memory_space=pl.ANY)],
        out_specs=pl.BlockSpec(memory_space=pl.ANY),
        scratch_shapes=[pltpu.VMEM((R, R), jnp.float32), pltpu.SemaphoreType.DMA(())],
        input_output_aliases={len(planes) + 1: 0},
        compiler_params=pltpu.CompilerParams(vmem_limit_bytes=VMEM_LIMIT),
        name="across",
    )(meta, *planes, sums)


def with_plane_before(f_ref, previous_ref):
    return previous_ref[...], f_ref[...]


def with_half_planes(low_ref, high_ref, after_low_ref, before_high_ref):
    left = jnp.concatenate([low_ref[...], before_high_ref[...]], axis=0)
    return left, jnp.concatenate([after_low_ref[...], high_ref[...]], axis=0)


def next_body(
    meta,
    f_ref,
    following_ref,
    previous_ref,
    theirs_ref,
    s_ref,
    density_ref,
    low_ref,
    high_ref,
):
    half = low_ref.shape[0]

    def put(value):
        low_ref[...] = value[:half, :]
        high_ref[...] = value[half:, :]

    def vector(k):
        return theirs_ref[3 * R + k : 3 * R + k + 1, :]

    def matrix(d):
        return theirs_ref[d * R : (d + 1) * R, :]

    @pl.when(meta[0] == 0)
    def _():
        f = f_ref[...]
        following = following_ref[...]
        previous = previous_ref[...]
        s = split(s_ref[...])
        out = dot3(split(f), split(KEEP * s_ref[...])) + GAIN * (density_ref[...] * vector(0))
        for d in range(3):
            plus, minus = unpack_speed(matrix(d), vector(d + 1))
            back = (previous, shifted_y(f, False), shifted_z(f, False))[d]
            ahead = (following, shifted_y(f, True), shifted_z(f, True))[d]
            change = dot3(split(f - back), split(dot3(s, split(plus))))
            change = change + dot3(split(ahead - f), split(dot3(s, split(minus))))
            out = out - time_step * change
        put(out)

    @pl.when(meta[0] == 1)
    def _():
        v0, v1, v2, maxwell = grid_speeds(meta, f_ref.shape[0], R)
        l = dot3(split(f_ref[...]), split(s_ref[...]), 1, 1)
        parts = split(l)
        out = KEEP * l + GAIN * (maxwell * vector(0))
        for d, v, positive in ((0, v0, first_sign(meta)), (1, v1, second_sign(meta))):
            e = matrix(d)
            out = out - time_step * (v * dot3(parts, split(jnp.where(positive, -e, e.T))))
        e = split(matrix(2))
        out = out + time_step * (jnp.maximum(v2, 0.0) * dot3(parts, e))
        put(out - time_step * (jnp.minimum(v2, 0.0) * dot3(parts, e, 1, 1)))


def second_body(total, meta, low_ref, high_ref, f_ref, density_ref, out_ref, k_ref):
    scale = 1.0 / total
    k = jnp.concatenate([low_ref[...], high_ref[...]], axis=0)
    k_ref[...] = k
    straight = k.T
    gram = dot(straight, k) * scale
    turned = split(straight)
    out_ref[:H, :] = gram[:H, :]
    out_ref[H:R, :H] = jnp.zeros((H, H), jnp.float32)
    out_ref[H:R, H:] = gram[H:, H:]

    def put_matrix(d, value):
        out_ref[(2 + d) * R : (3 + d) * R, :] = value

    def put_vector(i, value):
        out_ref[H + 2 * i : H + 2 * i + 1, :H] = value[:, :H]
        out_ref[H + 2 * i + 1 : H + 2 * i + 2, :H] = value[:, H:]

    put_matrix(-1, dot3(turned, split(f_ref[...])) * scale)

    @pl.when(meta[0] == 0)
    def _():
        put_matrix(0, jnp.zeros((R, R), jnp.float32))
        put_matrix(1, dot3(turned, split(shifted_y(k, True) - k)) * scale)
        put_matrix(2, dot3(turned, split(shifted_z(k, True) - k)) * scale)
        put_vector(0, (k * density_ref[...]).sum(axis=0, keepdims=True) * scale)

    @pl.when(meta[0] == 1)
    def _():
        put_speed_sums(meta, k, turned, gram, scale, put_matrix, put_vector)


def basis_body(meta, k_ref, inverse_ref, out_ref):
    out_ref[...] = dot(k_ref[...], inverse_ref[...].T)


def coefficient_body(
    meta,
    mine_ref,
    other_ref,
    inverse_ref,
    other_inverse_ref,
    s_ref,
    out_ref,
):
    def work(half, space_ref, speed_ref, pk_ref, pv_ref):
        def vector(ref, k):
            at = H + 2 * k
            return jnp.concatenate([ref[at : at + 1, :H], ref[at + 1 : at + 2, :H]], axis=1)

        pk, pv = pk_ref[...], pv_ref[...]
        rows = pk[half * H : (half + 1) * H, :]
        middle = dot(dot(space_ref[R : 2 * R, :], s_ref[...]), speed_ref[R : 2 * R, :], 1, 1)
        turned = dot(pk, middle)
        z = dot(dot(pk, turned, 0, 0), dot(pv, pv, 0, 0))
        row_parts = split(rows)
        parts = []
        for d in range(3):
            h = split(space_ref[(2 + d) * R : (3 + d) * R, :])
            parts += [dot3(row_parts, h), dot3(row_parts, h, 1, 1)]
        parts = dot3(split(jnp.concatenate(parts, axis=0)), split(z))
        change = jnp.zeros((H, R), jnp.float32)
        for d in range(3):
            packed = speed_ref[(2 + d) * R : (3 + d) * R, :]
            plus, minus = unpack_speed(packed, vector(speed_ref, d + 1))
            change = change + dot3(split(parts[2 * d * H : (2 * d + 1) * H, :]), split(minus))
            change = change - dot3(split(parts[(2 * d + 1) * H : (2 * d + 2) * H, :]), split(plus))
        xb = jnp.sum(rows * vector(space_ref, 0), axis=1, keepdims=True)
        out = KEEP * turned[half * H : (half + 1) * H, :] - time_step * change
        out = out + GAIN * (xb * vector(speed_ref, 0))
        out_ref[...] = dot(out, pv, 1, 1)

    @pl.when(meta[0] == 0)
    def _():
        work(0, mine_ref, other_ref, inverse_ref, other_inverse_ref)

    @pl.when(meta[0] == 1)
    def _():
        work(1, other_ref, mine_ref, other_inverse_ref, inverse_ref)


def step(factors, coefficients, density):
    rows_here = factors.shape[1]
    total = rows_here * lax.axis_size(AXES)
    start = lax.axis_index(AXES) * rows_here
    meta = jnp.stack([lax.axis_index("half"), start]).astype(jnp.int32)
    f = factors[0]
    column = density[:, None]

    half = rows_here // 2
    previous = to_neighbour(f, 1)
    following = to_neighbour(f, -1)

    sums = kernel_call(functools.partial(first_body, total), (4 * R, R), [f, column], meta)
    sums = add_across(0, total, with_plane_before, [f, previous], sums, meta)
    part = swap_halves(line_total(plane_scatter(sums)))
    part, following = lax.optimization_barrier((part, following))
    theirs = plane_gather(part)
    low, high = kernel_call(
        next_body, [(half, R)] * 2, [f, following, previous, theirs, coefficients, column], meta
    )

    before_high = to_neighbour(high, 1)
    after_low = to_neighbour(low, -1)
    sums, fresh = kernel_call(
        functools.partial(second_body, total),
        [(5 * R, R), (rows_here, R)],
        [low, high, f, column],
        meta,
    )
    sums = add_across(
        2 * R, total, with_half_planes, [low, high, after_low, before_high], sums, meta
    )
    mine = plane_gather(line_total(plane_scatter(sums)))
    other = swap_halves(mine)
    inverse = kernel_call(
        inverse_factor_body,
        (R, R),
        [mine],
        meta,
        [
            pltpu.VMEM((R, R), jnp.float32),
            pltpu.VMEM((B, B), jnp.float32),
            pltpu.VMEM((B // 8, 9, 8, 2 * B), jnp.float32),
            pltpu.VMEM((R, R), jnp.float32),
            pltpu.SemaphoreType.DMA(()),
        ],
        fetch=True,
    )
    basis = kernel_call(basis_body, (rows_here, R), [fresh, inverse], meta)
    other_inverse = swap_halves(inverse)
    updated = kernel_call(
        coefficient_body, (H, R), [mine, other, inverse, other_inverse, coefficients], meta
    )
    return (basis[None], updated)


def solution(mesh):
    torus = Mesh(mesh.devices.reshape(mesh.shape["half"], 4, 4, 4, 2), CELLS)
    return jax.shard_map(
        step,
        mesh=torus,
        in_specs=(P("half", AXES, None), P(), P(AXES)),
        out_specs=(P("half", AXES, None), P("half", None)),
        check_vma=False,
    )
```

```python
import functools

import jax
import jax.numpy as jnp
from jax import lax
from jax.experimental import pallas as pl
from jax.experimental.pallas import tpu as pltpu
from jax.sharding import Mesh
from jax.sharding import PartitionSpec as P

NZ = 32
VGRID = 64
R = 256
H = R // 2
VMEM_LIMIT = 20 << 20
AXES = ("y", "x", "zh", "zl")
PLANE = ("y", "x", "zl")
CELLS = ("half", "y", "x", "zh", "zl")

time_step = 0.2
relax_time = 0.5
KEEP = 1.0 - time_step / relax_time
GAIN = time_step / relax_time


def dot(a, b, ca=1, cb=0):
    return lax.dot_general(
        a,
        b,
        (((ca,), (cb,)), ((), ())),
        precision=lax.Precision.HIGHEST,
        preferred_element_type=jnp.float32,
    )


def split(x):
    high = x.astype(jnp.bfloat16)
    return high, (x - high.astype(jnp.float32)).astype(jnp.bfloat16)


def dot3(a, b, ca=1, cb=0):
    def part(x, y):
        return lax.dot_general(
            x, y, (((ca,), (cb,)), ((), ())), preferred_element_type=jnp.float32
        )

    return part(a[0], b[0]) + (part(a[0], b[1]) + part(a[1], b[0]))


def plane_scatter(x):
    parts = x.reshape(lax.axis_size(PLANE), -1, x.shape[1])
    return lax.all_to_all(parts, PLANE, 0, 0, tiled=True).sum(axis=0)


def plane_gather(part):
    size = lax.axis_size(PLANE)
    parts = lax.all_to_all(
        jnp.broadcast_to(part[None], (size, *part.shape)), PLANE, 0, 0, tiled=True
    )
    return parts.reshape(size * part.shape[0], part.shape[1])


def line_total(x):
    size = lax.axis_size("zh")

    def from_other(distance):
        return lax.ppermute(x, "zh", [(i, i ^ distance) for i in range(size)])

    parts = [x] + [from_other(distance) for distance in range(1, size)]
    while len(parts) > 1:
        parts = [parts[i] + parts[i + 1] for i in range(0, len(parts), 2)]
    return parts[0]


def swap_halves(x):
    return lax.ppermute(x, "half", [(0, 1), (1, 0)])


def to_neighbour(x, distance):
    count = lax.axis_size(AXES)
    return lax.ppermute(x, CELLS, [(i, (i + distance) % count) for i in range(count)])


def whole(count):
    return [pl.BlockSpec(memory_space=pltpu.VMEM)] * count


def kernel_call(body, out, arrays, meta, scratch=(), fetch=False):
    outs = out if isinstance(out, list) else [out]
    results = pl.pallas_call(
        body,
        out_shape=[jax.ShapeDtypeStruct(shape, jnp.float32) for shape in outs],
        in_specs=[pl.BlockSpec(memory_space=pltpu.SMEM)]
        + ([pl.BlockSpec(memory_space=pl.ANY)] * len(arrays) if fetch else whole(len(arrays))),
        out_specs=whole(len(outs)),
        scratch_shapes=list(scratch),
        compiler_params=pltpu.CompilerParams(vmem_limit_bytes=VMEM_LIMIT),
    )(meta, *arrays)
    return results if isinstance(out, list) else results[0]


B = 64


def block_inverse(d, out_ref, spread):
    rows = lax.broadcasted_iota(jnp.int32, (B, B), 0)
    cols = lax.broadcasted_iota(jnp.int32, (B, B), 1)
    eye = jnp.where(rows == cols, 1.0, 0.0).astype(jnp.float32)
    wide = jnp.concatenate([d, eye], axis=1)
    count = B // 8
    blk = [wide[8 * i : 8 * i + 8, :] for i in range(count)]
    sub = lax.broadcasted_iota(jnp.int32, (8, 2 * B), 0)

    def lane(v, j):
        return jnp.broadcast_to(v[:, j : j + 1], (8, 2 * B))

    def row(p, k, s):
        return spread[p, k, pl.ds(s, 8, stride=0), :]

    for p in range(count):
        cols_of = [[lane(blk[i], 8 * p + k) for k in range(8)] for i in range(p, count)]
        for k in range(8):
            spread[p, k, :, :] = cols_of[0][k]
        spread[p, 8, :, :] = blk[p]
        piv = {(a, b): row(p, b, a) for a in range(8) for b in range(a, 8)}
        r = [row(p, 8, a) for a in range(8)]
        done = blk[p]
        inv = {}
        for a in range(0, 8, 2):
            d00, d01, d11 = piv[a, a], piv[a, a + 1], piv[a + 1, a + 1]
            inv[a] = 1.0 / (d00 * d11 - d01 * d01)
            ratio = d01 / d00
            done = jnp.where(sub == a, r[a] * (1.0 / jnp.sqrt(d00)), done)
            last = (r[a + 1] - ratio * r[a]) * (1.0 / jnp.sqrt(d11 - ratio * d01))
            done = jnp.where(sub == a + 1, last, done)
            for b in range(a + 2, 8):
                e0, e1 = piv[a, b], piv[a + 1, b]
                t0 = (d11 * e0 - d01 * e1) * inv[a]
                t1 = (d00 * e1 - d01 * e0) * inv[a]
                for c in range(b, 8):
                    piv[b, c] = piv[b, c] - (t0 * piv[a, c] + t1 * piv[a + 1, c])
                r[b] = r[b] - (t0 * r[a] + t1 * r[a + 1])
        out_ref[8 * p : 8 * p + 8, :] = done[:, B:]
        if p + 1 < count:
            w = [None] * 8
            for a in (6, 4, 2, 0):
                y0, y1 = r[a], r[a + 1]
                for b in range(7, a + 1, -1):
                    y0 = y0 - piv[a, b] * w[b]
                    y1 = y1 - piv[a + 1, b] * w[b]
                d00, d01, d11 = piv[a, a], piv[a, a + 1], piv[a + 1, a + 1]
                w[a] = (d11 * y0 - d01 * y1) * inv[a]
                w[a + 1] = (d00 * y1 - d01 * y0) * inv[a]
            for i in range(p + 1, count):
                c = cols_of[i - p]
                even = (c[0] * w[0] + c[2] * w[2]) + (c[4] * w[4] + c[6] * w[6])
                odd = (c[1] * w[1] + c[3] * w[3]) + (c[5] * w[5] + c[7] * w[7])
                blk[i] = blk[i] - (even + odd)


def inverse_factor_body(meta, sums_ref, out_ref, work, small, spread, gram_ref, sem):
    copy = pltpu.make_async_copy(sums_ref.at[pl.ds(0, R), :], gram_ref, sem)
    copy.start()
    copy.wait()
    rows = lax.broadcasted_iota(jnp.int32, (R, R), 0)
    cols = lax.broadcasted_iota(jnp.int32, (R, R), 1)
    work[:H, :] = gram_ref[:H, :]
    work[H:, :H] = gram_ref[:H, H:].T
    work[H:, H:] = gram_ref[H:R, H:]
    g = work[...]
    diag = jnp.where(rows == cols, g, 0.0)
    across = 1.0 / jnp.sqrt(jnp.sum(diag, axis=0, keepdims=True))
    down = 1.0 / jnp.sqrt(jnp.sum(diag, axis=1, keepdims=True))
    work[...] = g * across * down
    for k in range(R // B):
        lo, hi = k * B, (k + 1) * B
        block_inverse(work[lo:hi, lo:hi], small, spread)
        ik = small[...]
        left = dot(ik, work[lo:hi, :])
        ccols = lax.broadcasted_iota(jnp.int32, (B, R), 1)
        wide = jnp.concatenate([ik] * (R // B), axis=1)
        panel = jnp.where((ccols >= lo) & (ccols < hi), wide, left)
        work[lo:hi, :] = panel
        if hi < R:
            at = hi // 128 * 128
            update = dot(left[:, at:], panel, 0, 0)
            below = work[hi:, :]
            bcols = lax.broadcasted_iota(jnp.int32, (R - hi, R), 1)
            below = jnp.where((bcols >= lo) & (bcols < hi), 0.0, below)
            work[hi:, :] = below - update[hi - at :, :]
    out_ref[...] = jnp.where(rows >= cols, work[...], 0.0) * across


def upper_mask():
    return lax.broadcasted_iota(jnp.int32, (R, R), 0) <= lax.broadcasted_iota(jnp.int32, (R, R), 1)


def diagonal_mask():
    return lax.broadcasted_iota(jnp.int32, (R, R), 0) == lax.broadcasted_iota(jnp.int32, (R, R), 1)


def shifted_y(x, forward):
    if forward:
        return jnp.concatenate([x[NZ:], x[:NZ]], axis=0)
    return jnp.concatenate([x[-NZ:], x[:-NZ]], axis=0)


def shifted_z(x, forward):
    count = x.shape[0]
    place = lax.broadcasted_iota(jnp.int32, x.shape, 0) & (NZ - 1)
    if forward:
        return jnp.where(
            place == NZ - 1, pltpu.roll(x, NZ - 1, 0), pltpu.roll(x, count - 1, 0)
        )
    return jnp.where(place == 0, pltpu.roll(x, count - NZ + 1, 0), pltpu.roll(x, 1, 0))


def grid_speeds(meta, count, width):
    start = meta[1]
    row = lax.broadcasted_iota(jnp.int32, (count, width), 0)
    third = (row & (NZ - 1)).astype(jnp.float32)
    second = ((start // NZ) % VGRID + row // NZ).astype(jnp.float32)
    first = (start // (NZ * VGRID)).astype(jnp.float32)
    v0 = -1.0 + (2.0 * first + 1.0) / VGRID
    v1 = -1.0 + (2.0 * second + 1.0) / VGRID
    v2 = -1.0 + (2.0 * third + 1.0) / NZ
    maxwell = jnp.exp(-2.0 * (v0 * v0 + v1 * v1 + v2 * v2))
    return v0, v1, v2, maxwell


def first_sign(meta):
    return meta[1] // (NZ * VGRID) >= VGRID // 2


def second_sign(meta):
    return (meta[1] // NZ) % VGRID >= VGRID // 2


def unpack_speed(packed, diag):
    upper, diagonal = upper_mask(), diagonal_mask()
    flipped = packed.T
    plus = jnp.where(upper, packed, flipped)
    minus = jnp.where(diagonal, diag, jnp.where(upper, flipped, packed))
    return plus, minus


def put_speed_sums(meta, f, turned, gram, scale, put_matrix, put_vector):
    upper, diagonal = upper_mask(), diagonal_mask()
    v0, v1, v2, maxwell = grid_speeds(meta, f.shape[0], R)

    def one_sign(d, value, positive):
        low = jnp.where(upper, 0.0, value)
        high = jnp.where(upper, value, 0.0)
        put_matrix(d, jnp.where(positive, high, low))
        diag = jnp.where(diagonal, value, 0.0).sum(axis=0, keepdims=True)
        put_vector(d + 1, jnp.where(positive, 0.0, diag))

    one_sign(0, v0 * gram, first_sign(meta))
    one_sign(1, dot3(turned, split(v1 * f)) * scale, second_sign(meta))
    plus = dot3(turned, split(jnp.maximum(v2, 0.0) * f)) * scale
    minus = dot3(turned, split(jnp.minimum(v2, 0.0) * f)) * scale
    put_matrix(2, jnp.where(upper, plus, minus))
    put_vector(3, jnp.where(diagonal, minus, 0.0).sum(axis=0, keepdims=True))
    put_vector(0, (f * maxwell).sum(axis=0, keepdims=True) * scale)


def first_body(total, meta, f_ref, density_ref, out_ref):
    scale = 1.0 / total
    out_ref[3 * R :, :] = jnp.zeros((R, R), jnp.float32)

    def put_vector(k, value):
        out_ref[3 * R + k : 3 * R + k + 1, :] = value

    def put_matrix(d, value):
        out_ref[d * R : (d + 1) * R, :] = value

    f = f_ref[...]
    turned = split(f.T)

    @pl.when(meta[0] == 0)
    def _():
        put_matrix(0, jnp.zeros((R, R), jnp.float32))
        put_matrix(1, dot3(turned, split(shifted_y(f, True) - f)) * scale)
        put_matrix(2, dot3(turned, split(shifted_z(f, True) - f)) * scale)
        put_vector(0, (f * density_ref[...]).sum(axis=0, keepdims=True) * scale)

    @pl.when(meta[0] == 1)
    def _():
        gram = dot3(turned, split(f)) * scale
        put_speed_sums(meta, f, turned, gram, scale, put_matrix, put_vector)


def across_body(at, total, pairs, meta, *refs):
    *planes, sums_ref, out_ref, block, sem = refs
    del sums_ref

    @pl.when(meta[0] == 0)
    def _():
        left, right = pairs(*planes)
        block[...] = dot3(split(left.T), split(right - left)) * (1.0 / total)
        copy = pltpu.make_async_copy(block, out_ref.at[pl.ds(at, R), :], sem)
        copy.start()
        copy.wait()


def add_across(at, total, pairs, planes, sums, meta):
    return pl.pallas_call(
        functools.partial(across_body, at, total, pairs),
        out_shape=jax.ShapeDtypeStruct(sums.shape, jnp.float32),
        in_specs=[pl.BlockSpec(memory_space=pltpu.SMEM)]
        + whole(len(planes))
        + [pl.BlockSpec(memory_space=pl.ANY)],
        out_specs=pl.BlockSpec(memory_space=pl.ANY),
        scratch_shapes=[pltpu.VMEM((R, R), jnp.float32), pltpu.SemaphoreType.DMA(())],
        input_output_aliases={len(planes) + 1: 0},
        compiler_params=pltpu.CompilerParams(vmem_limit_bytes=VMEM_LIMIT),
        name="across",
    )(meta, *planes, sums)


def with_plane_before(f_ref, previous_ref):
    return previous_ref[...], f_ref[...]


def with_half_planes(low_ref, high_ref, after_low_ref, before_high_ref):
    left = jnp.concatenate([low_ref[...], before_high_ref[...]], axis=0)
    return left, jnp.concatenate([after_low_ref[...], high_ref[...]], axis=0)


def next_body(
    meta,
    f_ref,
    following_ref,
    previous_ref,
    theirs_ref,
    s_ref,
    density_ref,
    low_ref,
    high_ref,
):
    half = low_ref.shape[0]

    def put(value):
        low_ref[...] = value[:half, :]
        high_ref[...] = value[half:, :]

    def vector(k):
        return theirs_ref[3 * R + k : 3 * R + k + 1, :]

    def matrix(d):
        return theirs_ref[d * R : (d + 1) * R, :]

    @pl.when(meta[0] == 0)
    def _():
        f = f_ref[...]
        following = following_ref[...]
        previous = previous_ref[...]
        s = split(s_ref[...])
        out = dot3(split(f), split(KEEP * s_ref[...])) + GAIN * (density_ref[...] * vector(0))
        for d in range(3):
            plus, minus = unpack_speed(matrix(d), vector(d + 1))
            back = (previous, shifted_y(f, False), shifted_z(f, False))[d]
            ahead = (following, shifted_y(f, True), shifted_z(f, True))[d]
            change = dot3(split(f - back), split(dot3(s, split(plus))))
            change = change + dot3(split(ahead - f), split(dot3(s, split(minus))))
            out = out - time_step * change
        put(out)

    @pl.when(meta[0] == 1)
    def _():
        v0, v1, v2, maxwell = grid_speeds(meta, f_ref.shape[0], R)
        l = dot3(split(f_ref[...]), split(s_ref[...]), 1, 1)
        parts = split(l)
        out = KEEP * l + GAIN * (maxwell * vector(0))
        for d, v, positive in ((0, v0, first_sign(meta)), (1, v1, second_sign(meta))):
            e = matrix(d)
            out = out - time_step * (v * dot3(parts, split(jnp.where(positive, -e, e.T))))
        e = split(matrix(2))
        out = out + time_step * (jnp.maximum(v2, 0.0) * dot3(parts, e))
        put(out - time_step * (jnp.minimum(v2, 0.0) * dot3(parts, e, 1, 1)))


def second_body(total, meta, low_ref, high_ref, f_ref, density_ref, out_ref, k_ref):
    scale = 1.0 / total
    k = jnp.concatenate([low_ref[...], high_ref[...]], axis=0)
    k_ref[...] = k
    straight = k.T
    gram = dot(straight, k) * scale
    turned = split(straight)
    out_ref[:H, :] = gram[:H, :]
    out_ref[H:R, :H] = jnp.zeros((H, H), jnp.float32)
    out_ref[H:R, H:] = gram[H:, H:]

    def put_matrix(d, value):
        out_ref[(2 + d) * R : (3 + d) * R, :] = value

    def put_vector(i, value):
        out_ref[H + 2 * i : H + 2 * i + 1, :H] = value[:, :H]
        out_ref[H + 2 * i + 1 : H + 2 * i + 2, :H] = value[:, H:]

    put_matrix(-1, dot3(turned, split(f_ref[...])) * scale)

    @pl.when(meta[0] == 0)
    def _():
        put_matrix(0, jnp.zeros((R, R), jnp.float32))
        put_matrix(1, dot3(turned, split(shifted_y(k, True) - k)) * scale)
        put_matrix(2, dot3(turned, split(shifted_z(k, True) - k)) * scale)
        put_vector(0, (k * density_ref[...]).sum(axis=0, keepdims=True) * scale)

    @pl.when(meta[0] == 1)
    def _():
        put_speed_sums(meta, k, turned, gram, scale, put_matrix, put_vector)


def basis_body(meta, k_ref, inverse_ref, out_ref):
    out_ref[...] = dot(k_ref[...], inverse_ref[...].T)


def coefficient_body(
    meta,
    mine_ref,
    other_ref,
    inverse_ref,
    other_inverse_ref,
    s_ref,
    out_ref,
):
    def work(half, space_ref, speed_ref, pk_ref, pv_ref):
        def vector(ref, k):
            at = H + 2 * k
            return jnp.concatenate([ref[at : at + 1, :H], ref[at + 1 : at + 2, :H]], axis=1)

        pk, pv = pk_ref[...], pv_ref[...]
        rows = pk[half * H : (half + 1) * H, :]
        middle = dot(dot(space_ref[R : 2 * R, :], s_ref[...]), speed_ref[R : 2 * R, :], 1, 1)
        turned = dot(pk, middle)
        z = dot(dot(pk, turned, 0, 0), dot(pv, pv, 0, 0))
        row_parts = split(rows)
        parts = []
        for d in range(3):
            h = split(space_ref[(2 + d) * R : (3 + d) * R, :])
            parts += [dot3(row_parts, h), dot3(row_parts, h, 1, 1)]
        parts = dot3(split(jnp.concatenate(parts, axis=0)), split(z))
        change = jnp.zeros((H, R), jnp.float32)
        for d in range(3):
            packed = speed_ref[(2 + d) * R : (3 + d) * R, :]
            plus, minus = unpack_speed(packed, vector(speed_ref, d + 1))
            change = change + dot3(split(parts[2 * d * H : (2 * d + 1) * H, :]), split(minus))
            change = change - dot3(split(parts[(2 * d + 1) * H : (2 * d + 2) * H, :]), split(plus))
        xb = jnp.sum(rows * vector(space_ref, 0), axis=1, keepdims=True)
        out = KEEP * turned[half * H : (half + 1) * H, :] - time_step * change
        out = out + GAIN * (xb * vector(speed_ref, 0))
        out_ref[...] = dot(out, pv, 1, 1)

    @pl.when(meta[0] == 0)
    def _():
        work(0, mine_ref, other_ref, inverse_ref, other_inverse_ref)

    @pl.when(meta[0] == 1)
    def _():
        work(1, other_ref, mine_ref, other_inverse_ref, inverse_ref)


def step(factors, coefficients, density):
    rows_here = factors.shape[1]
    total = rows_here * lax.axis_size(AXES)
    start = lax.axis_index(AXES) * rows_here
    meta = jnp.stack([lax.axis_index("half"), start]).astype(jnp.int32)
    f = factors[0]
    column = density[:, None]

    half = rows_here // 2
    previous = to_neighbour(f, 1)
    following = to_neighbour(f, -1)

    sums = kernel_call(functools.partial(first_body, total), (4 * R, R), [f, column], meta)
    sums = add_across(0, total, with_plane_before, [f, previous], sums, meta)
    part = swap_halves(line_total(plane_scatter(sums)))
    part, following = lax.optimization_barrier((part, following))
    theirs = plane_gather(part)
    low, high = kernel_call(
        next_body, [(half, R)] * 2, [f, following, previous, theirs, coefficients, column], meta
    )

    before_high = to_neighbour(high, 1)
    after_low = to_neighbour(low, -1)
    sums, fresh = kernel_call(
        functools.partial(second_body, total),
        [(5 * R, R), (rows_here, R)],
        [low, high, f, column],
        meta,
    )
    sums = add_across(
        2 * R, total, with_half_planes, [low, high, after_low, before_high], sums, meta
    )
    mine = plane_gather(line_total(plane_scatter(sums)))
    other = swap_halves(mine)
    inverse = kernel_call(
        inverse_factor_body,
        (R, R),
        [mine],
        meta,
        [
            pltpu.VMEM((R, R), jnp.float32),
            pltpu.VMEM((B, B), jnp.float32),
            pltpu.VMEM((B // 8, 9, 8, 2 * B), jnp.float32),
            pltpu.VMEM((R, R), jnp.float32),
            pltpu.SemaphoreType.DMA(()),
        ],
        fetch=True,
    )
    basis = kernel_call(basis_body, (rows_here, R), [fresh, inverse], meta)
    other_inverse = swap_halves(inverse)
    updated = kernel_call(
        coefficient_body, (H, R), [mine, other, inverse, other_inverse, coefficients], meta
    )
    return (basis[None], updated)


def solution(mesh):
    torus = Mesh(mesh.devices.reshape(mesh.shape["half"], 4, 4, 4, 2), CELLS)
    return jax.shard_map(
        step,
        mesh=torus,
        in_specs=(P("half", AXES, None), P(), P(AXES)),
        out_specs=(P("half", AXES, None), P("half", None)),
        check_vma=False,
    )
```

```python
import functools

import jax
import jax.numpy as jnp
from jax import lax
from jax.experimental import pallas as pl
from jax.experimental.pallas import tpu as pltpu
from jax.sharding import Mesh
from jax.sharding import PartitionSpec as P

NZ = 32
VGRID = 64
R = 256
H = R // 2
VMEM_LIMIT = 20 << 20
AXES = ("y", "x", "zh", "zl")
PLANE = ("y", "x", "zl")
CELLS = ("half", "y", "x", "zh", "zl")

time_step = 0.2
relax_time = 0.5
KEEP = 1.0 - time_step / relax_time
GAIN = time_step / relax_time


def dot(a, b, ca=1, cb=0):
    return lax.dot_general(
        a,
        b,
        (((ca,), (cb,)), ((), ())),
        precision=lax.Precision.HIGHEST,
        preferred_element_type=jnp.float32,
    )


def split(x):
    high = x.astype(jnp.bfloat16)
    return high, (x - high.astype(jnp.float32)).astype(jnp.bfloat16)


def dot3(a, b, ca=1, cb=0):
    def part(x, y):
        return lax.dot_general(
            x, y, (((ca,), (cb,)), ((), ())), preferred_element_type=jnp.float32
        )

    return part(a[0], b[0]) + (part(a[0], b[1]) + part(a[1], b[0]))


def plane_scatter(x):
    parts = x.reshape(lax.axis_size(PLANE), -1, x.shape[1])
    return lax.all_to_all(parts, PLANE, 0, 0, tiled=True).sum(axis=0)


def plane_gather(part):
    size = lax.axis_size(PLANE)
    parts = lax.all_to_all(
        jnp.broadcast_to(part[None], (size, *part.shape)), PLANE, 0, 0, tiled=True
    )
    return parts.reshape(size * part.shape[0], part.shape[1])


def line_total(x):
    size = lax.axis_size("zh")

    def from_other(distance):
        return lax.ppermute(x, "zh", [(i, i ^ distance) for i in range(size)])

    parts = [x] + [from_other(distance) for distance in range(1, size)]
    while len(parts) > 1:
        parts = [parts[i] + parts[i + 1] for i in range(0, len(parts), 2)]
    return parts[0]


def swap_halves(x):
    return lax.ppermute(x, "half", [(0, 1), (1, 0)])


def to_neighbour(x, distance):
    count = lax.axis_size(AXES)
    return lax.ppermute(x, CELLS, [(i, (i + distance) % count) for i in range(count)])


def whole(count):
    return [pl.BlockSpec(memory_space=pltpu.VMEM)] * count


def kernel_call(body, out, arrays, meta, scratch=(), fetch=False):
    outs = out if isinstance(out, list) else [out]
    results = pl.pallas_call(
        body,
        out_shape=[jax.ShapeDtypeStruct(shape, jnp.float32) for shape in outs],
        in_specs=[pl.BlockSpec(memory_space=pltpu.SMEM)]
        + ([pl.BlockSpec(memory_space=pl.ANY)] * len(arrays) if fetch else whole(len(arrays))),
        out_specs=whole(len(outs)),
        scratch_shapes=list(scratch),
        compiler_params=pltpu.CompilerParams(vmem_limit_bytes=VMEM_LIMIT),
    )(meta, *arrays)
    return results if isinstance(out, list) else results[0]


B = 64


def block_inverse(d, out_ref, spread):
    rows = lax.broadcasted_iota(jnp.int32, (B, B), 0)
    cols = lax.broadcasted_iota(jnp.int32, (B, B), 1)
    eye = jnp.where(rows == cols, 1.0, 0.0).astype(jnp.float32)
    wide = jnp.concatenate([d, eye], axis=1)
    count = B // 8
    blk = [wide[8 * i : 8 * i + 8, :] for i in range(count)]
    sub = lax.broadcasted_iota(jnp.int32, (8, 2 * B), 0)

    def lane(v, j):
        return jnp.broadcast_to(v[:, j : j + 1], (8, 2 * B))

    def row(p, k, s):
        return spread[p, k, pl.ds(s, 8, stride=0), :]

    for p in range(count):
        cols_of = [[lane(blk[i], 8 * p + k) for k in range(8)] for i in range(p, count)]
        for k in range(8):
            spread[p, k, :, :] = cols_of[0][k]
        spread[p, 8, :, :] = blk[p]
        piv = {(a, b): row(p, b, a) for a in range(8) for b in range(a, 8)}
        r = [row(p, 8, a) for a in range(8)]
        done = blk[p]
        inv = {}
        for a in range(0, 8, 2):
            d00, d01, d11 = piv[a, a], piv[a, a + 1], piv[a + 1, a + 1]
            inv[a] = 1.0 / (d00 * d11 - d01 * d01)
            ratio = d01 / d00
            done = jnp.where(sub == a, r[a] * (1.0 / jnp.sqrt(d00)), done)
            last = (r[a + 1] - ratio * r[a]) * (1.0 / jnp.sqrt(d11 - ratio * d01))
            done = jnp.where(sub == a + 1, last, done)
            for b in range(a + 2, 8):
                e0, e1 = piv[a, b], piv[a + 1, b]
                t0 = (d11 * e0 - d01 * e1) * inv[a]
                t1 = (d00 * e1 - d01 * e0) * inv[a]
                for c in range(b, 8):
                    piv[b, c] = piv[b, c] - (t0 * piv[a, c] + t1 * piv[a + 1, c])
                r[b] = r[b] - (t0 * r[a] + t1 * r[a + 1])
        out_ref[8 * p : 8 * p + 8, :] = done[:, B:]
        if p + 1 < count:
            w = [None] * 8
            for a in (6, 4, 2, 0):
                y0, y1 = r[a], r[a + 1]
                for b in range(7, a + 1, -1):
                    y0 = y0 - piv[a, b] * w[b]
                    y1 = y1 - piv[a + 1, b] * w[b]
                d00, d01, d11 = piv[a, a], piv[a, a + 1], piv[a + 1, a + 1]
                w[a] = (d11 * y0 - d01 * y1) * inv[a]
                w[a + 1] = (d00 * y1 - d01 * y0) * inv[a]
            for i in range(p + 1, count):
                c = cols_of[i - p]
                even = (c[0] * w[0] + c[2] * w[2]) + (c[4] * w[4] + c[6] * w[6])
                odd = (c[1] * w[1] + c[3] * w[3]) + (c[5] * w[5] + c[7] * w[7])
                blk[i] = blk[i] - (even + odd)


def inverse_factor_body(meta, sums_ref, out_ref, work, small, spread, gram_ref, sem):
    copy = pltpu.make_async_copy(sums_ref.at[pl.ds(0, R), :], gram_ref, sem)
    copy.start()
    copy.wait()
    rows = lax.broadcasted_iota(jnp.int32, (R, R), 0)
    cols = lax.broadcasted_iota(jnp.int32, (R, R), 1)
    work[:H, :] = gram_ref[:H, :]
    work[H:, :H] = gram_ref[:H, H:].T
    work[H:, H:] = gram_ref[H:R, H:]
    g = work[...]
    diag = jnp.where(rows == cols, g, 0.0)
    across = 1.0 / jnp.sqrt(jnp.sum(diag, axis=0, keepdims=True))
    down = 1.0 / jnp.sqrt(jnp.sum(diag, axis=1, keepdims=True))
    work[...] = g * across * down
    for k in range(R // B):
        lo, hi = k * B, (k + 1) * B
        block_inverse(work[lo:hi, lo:hi], small, spread)
        ik = small[...]
        left = dot(ik, work[lo:hi, :])
        ccols = lax.broadcasted_iota(jnp.int32, (B, R), 1)
        wide = jnp.concatenate([ik] * (R // B), axis=1)
        panel = jnp.where((ccols >= lo) & (ccols < hi), wide, left)
        work[lo:hi, :] = panel
        if hi < R:
            at = hi // 128 * 128
            update = dot(left[:, at:], panel, 0, 0)
            below = work[hi:, :]
            bcols = lax.broadcasted_iota(jnp.int32, (R - hi, R), 1)
            below = jnp.where((bcols >= lo) & (bcols < hi), 0.0, below)
            work[hi:, :] = below - update[hi - at :, :]
    out_ref[...] = jnp.where(rows >= cols, work[...], 0.0) * across


def upper_mask():
    return lax.broadcasted_iota(jnp.int32, (R, R), 0) <= lax.broadcasted_iota(jnp.int32, (R, R), 1)


def diagonal_mask():
    return lax.broadcasted_iota(jnp.int32, (R, R), 0) == lax.broadcasted_iota(jnp.int32, (R, R), 1)


def shifted_y(x, forward):
    if forward:
        return jnp.concatenate([x[NZ:], x[:NZ]], axis=0)
    return jnp.concatenate([x[-NZ:], x[:-NZ]], axis=0)


def shifted_z(x, forward):
    count = x.shape[0]
    place = lax.broadcasted_iota(jnp.int32, x.shape, 0) & (NZ - 1)
    if forward:
        return jnp.where(
            place == NZ - 1, pltpu.roll(x, NZ - 1, 0), pltpu.roll(x, count - 1, 0)
        )
    return jnp.where(place == 0, pltpu.roll(x, count - NZ + 1, 0), pltpu.roll(x, 1, 0))


def grid_speeds(meta, count, width):
    start = meta[1]
    row = lax.broadcasted_iota(jnp.int32, (count, width), 0)
    third = (row & (NZ - 1)).astype(jnp.float32)
    second = ((start // NZ) % VGRID + row // NZ).astype(jnp.float32)
    first = (start // (NZ * VGRID)).astype(jnp.float32)
    v0 = -1.0 + (2.0 * first + 1.0) / VGRID
    v1 = -1.0 + (2.0 * second + 1.0) / VGRID
    v2 = -1.0 + (2.0 * third + 1.0) / NZ
    maxwell = jnp.exp(-2.0 * (v0 * v0 + v1 * v1 + v2 * v2))
    return v0, v1, v2, maxwell


def first_sign(meta):
    return meta[1] // (NZ * VGRID) >= VGRID // 2


def second_sign(meta):
    return (meta[1] // NZ) % VGRID >= VGRID // 2


def unpack_speed(packed, diag):
    upper, diagonal = upper_mask(), diagonal_mask()
    flipped = packed.T
    plus = jnp.where(upper, packed, flipped)
    minus = jnp.where(diagonal, diag, jnp.where(upper, flipped, packed))
    return plus, minus


def put_speed_sums(meta, f, turned, gram, scale, put_matrix, put_vector):
    upper, diagonal = upper_mask(), diagonal_mask()
    v0, v1, v2, maxwell = grid_speeds(meta, f.shape[0], R)

    def one_sign(d, value, positive):
        low = jnp.where(upper, 0.0, value)
        high = jnp.where(upper, value, 0.0)
        put_matrix(d, jnp.where(positive, high, low))
        diag = jnp.where(diagonal, value, 0.0).sum(axis=0, keepdims=True)
        put_vector(d + 1, jnp.where(positive, 0.0, diag))

    one_sign(0, v0 * gram, first_sign(meta))
    one_sign(1, dot3(turned, split(v1 * f)) * scale, second_sign(meta))
    plus = dot3(turned, split(jnp.maximum(v2, 0.0) * f)) * scale
    minus = dot3(turned, split(jnp.minimum(v2, 0.0) * f)) * scale
    put_matrix(2, jnp.where(upper, plus, minus))
    put_vector(3, jnp.where(diagonal, minus, 0.0).sum(axis=0, keepdims=True))
    put_vector(0, (f * maxwell).sum(axis=0, keepdims=True) * scale)


def first_body(total, meta, f_ref, density_ref, out_ref):
    scale = 1.0 / total
    out_ref[3 * R :, :] = jnp.zeros((R, R), jnp.float32)

    def put_vector(k, value):
        out_ref[3 * R + k : 3 * R + k + 1, :] = value

    def put_matrix(d, value):
        out_ref[d * R : (d + 1) * R, :] = value

    f = f_ref[...]
    turned = split(f.T)

    @pl.when(meta[0] == 0)
    def _():
        put_matrix(0, jnp.zeros((R, R), jnp.float32))
        put_matrix(1, dot3(turned, split(shifted_y(f, True) - f)) * scale)
        put_matrix(2, dot3(turned, split(shifted_z(f, True) - f)) * scale)
        put_vector(0, (f * density_ref[...]).sum(axis=0, keepdims=True) * scale)

    @pl.when(meta[0] == 1)
    def _():
        gram = dot3(turned, split(f)) * scale
        put_speed_sums(meta, f, turned, gram, scale, put_matrix, put_vector)


def across_body(at, total, pairs, meta, *refs):
    *planes, sums_ref, out_ref, block, sem = refs
    del sums_ref

    @pl.when(meta[0] == 0)
    def _():
        left, right = pairs(*planes)
        block[...] = dot3(split(left.T), split(right - left)) * (1.0 / total)
        copy = pltpu.make_async_copy(block, out_ref.at[pl.ds(at, R), :], sem)
        copy.start()
        copy.wait()


def add_across(at, total, pairs, planes, sums, meta):
    return pl.pallas_call(
        functools.partial(across_body, at, total, pairs),
        out_shape=jax.ShapeDtypeStruct(sums.shape, jnp.float32),
        in_specs=[pl.BlockSpec(memory_space=pltpu.SMEM)]
        + whole(len(planes))
        + [pl.BlockSpec(memory_space=pl.ANY)],
        out_specs=pl.BlockSpec(memory_space=pl.ANY),
        scratch_shapes=[pltpu.VMEM((R, R), jnp.float32), pltpu.SemaphoreType.DMA(())],
        input_output_aliases={len(planes) + 1: 0},
        compiler_params=pltpu.CompilerParams(vmem_limit_bytes=VMEM_LIMIT),
        name="across",
    )(meta, *planes, sums)


def with_plane_before(f_ref, previous_ref):
    return previous_ref[...], f_ref[...]


def with_half_planes(low_ref, high_ref, after_low_ref, before_high_ref):
    left = jnp.concatenate([low_ref[...], before_high_ref[...]], axis=0)
    return left, jnp.concatenate([after_low_ref[...], high_ref[...]], axis=0)


def next_body(
    meta,
    f_ref,
    following_ref,
    previous_ref,
    theirs_ref,
    s_ref,
    density_ref,
    low_ref,
    high_ref,
):
    half = low_ref.shape[0]

    def put(value):
        low_ref[...] = value[:half, :]
        high_ref[...] = value[half:, :]

    def vector(k):
        return theirs_ref[3 * R + k : 3 * R + k + 1, :]

    def matrix(d):
        return theirs_ref[d * R : (d + 1) * R, :]

    @pl.when(meta[0] == 0)
    def _():
        f = f_ref[...]
        following = following_ref[...]
        previous = previous_ref[...]
        s = split(s_ref[...])
        out = dot3(split(f), split(KEEP * s_ref[...])) + GAIN * (density_ref[...] * vector(0))
        for d in range(3):
            plus, minus = unpack_speed(matrix(d), vector(d + 1))
            back = (previous, shifted_y(f, False), shifted_z(f, False))[d]
            ahead = (following, shifted_y(f, True), shifted_z(f, True))[d]
            change = dot3(split(f - back), split(dot3(s, split(plus))))
            change = change + dot3(split(ahead - f), split(dot3(s, split(minus))))
            out = out - time_step * change
        put(out)

    @pl.when(meta[0] == 1)
    def _():
        v0, v1, v2, maxwell = grid_speeds(meta, f_ref.shape[0], R)
        l = dot3(split(f_ref[...]), split(s_ref[...]), 1, 1)
        parts = split(l)
        out = KEEP * l + GAIN * (maxwell * vector(0))
        for d, v, positive in ((0, v0, first_sign(meta)), (1, v1, second_sign(meta))):
            e = matrix(d)
            out = out - time_step * (v * dot3(parts, split(jnp.where(positive, -e, e.T))))
        e = split(matrix(2))
        out = out + time_step * (jnp.maximum(v2, 0.0) * dot3(parts, e))
        put(out - time_step * (jnp.minimum(v2, 0.0) * dot3(parts, e, 1, 1)))


def second_body(total, meta, low_ref, high_ref, f_ref, density_ref, out_ref, k_ref):
    scale = 1.0 / total
    k = jnp.concatenate([low_ref[...], high_ref[...]], axis=0)
    k_ref[...] = k
    straight = k.T
    gram = dot(straight, k) * scale
    turned = split(straight)
    out_ref[:H, :] = gram[:H, :]
    out_ref[H:R, :H] = jnp.zeros((H, H), jnp.float32)
    out_ref[H:R, H:] = gram[H:, H:]

    def put_matrix(d, value):
        out_ref[(2 + d) * R : (3 + d) * R, :] = value

    def put_vector(i, value):
        out_ref[H + 2 * i : H + 2 * i + 1, :H] = value[:, :H]
        out_ref[H + 2 * i + 1 : H + 2 * i + 2, :H] = value[:, H:]

    put_matrix(-1, dot3(turned, split(f_ref[...])) * scale)

    @pl.when(meta[0] == 0)
    def _():
        put_matrix(0, jnp.zeros((R, R), jnp.float32))
        put_matrix(1, dot3(turned, split(shifted_y(k, True) - k)) * scale)
        put_matrix(2, dot3(turned, split(shifted_z(k, True) - k)) * scale)
        put_vector(0, (k * density_ref[...]).sum(axis=0, keepdims=True) * scale)

    @pl.when(meta[0] == 1)
    def _():
        put_speed_sums(meta, k, turned, gram, scale, put_matrix, put_vector)


def basis_body(meta, k_ref, inverse_ref, out_ref):
    out_ref[...] = dot(k_ref[...], inverse_ref[...].T)


def coefficient_body(
    meta,
    mine_ref,
    other_ref,
    inverse_ref,
    other_inverse_ref,
    s_ref,
    out_ref,
    space_ref,
    speed_ref,
    pk_ref,
    pv_ref,
):
    @pl.when(meta[0] == 0)
    def _():
        space_ref[...] = mine_ref[...]
        speed_ref[...] = other_ref[...]
        pk_ref[...] = inverse_ref[...]
        pv_ref[...] = other_inverse_ref[...]

    @pl.when(meta[0] == 1)
    def _():
        space_ref[...] = other_ref[...]
        speed_ref[...] = mine_ref[...]
        pk_ref[...] = other_inverse_ref[...]
        pv_ref[...] = inverse_ref[...]

    def work():
        def vector(ref, k):
            at = H + 2 * k
            return jnp.concatenate([ref[at : at + 1, :H], ref[at + 1 : at + 2, :H]], axis=1)

        pk, pv = pk_ref[...], pv_ref[...]
        rows = pk_ref[pl.ds(pl.multiple_of(meta[0] * H, H), H), :]
        middle = dot(dot(space_ref[R : 2 * R, :], s_ref[...]), speed_ref[R : 2 * R, :], 1, 1)
        turned = dot(pk, middle)
        z = dot(dot(pk, turned, 0, 0), dot(pv, pv, 0, 0))
        row_parts = split(rows)
        parts = []
        for d in range(3):
            h = split(space_ref[(2 + d) * R : (3 + d) * R, :])
            parts += [dot3(row_parts, h), dot3(row_parts, h, 1, 1)]
        parts = dot3(split(jnp.concatenate(parts, axis=0)), split(z))
        change = jnp.zeros((H, R), jnp.float32)
        for d in range(3):
            packed = speed_ref[(2 + d) * R : (3 + d) * R, :]
            plus, minus = unpack_speed(packed, vector(speed_ref, d + 1))
            change = change + dot3(split(parts[2 * d * H : (2 * d + 1) * H, :]), split(minus))
            change = change - dot3(split(parts[(2 * d + 1) * H : (2 * d + 2) * H, :]), split(plus))
        xb = jnp.sum(rows * vector(space_ref, 0), axis=1, keepdims=True)
        own_turned = jnp.where(meta[0] == 0, turned[:H, :], turned[H:, :])
        out = KEEP * own_turned - time_step * change
        out = out + GAIN * (xb * vector(speed_ref, 0))
        out_ref[...] = dot(out, pv, 1, 1)

    work()


def step(factors, coefficients, density):
    rows_here = factors.shape[1]
    total = rows_here * lax.axis_size(AXES)
    start = lax.axis_index(AXES) * rows_here
    meta = jnp.stack([lax.axis_index("half"), start]).astype(jnp.int32)
    f = factors[0]
    column = density[:, None]

    half = rows_here // 2
    previous = to_neighbour(f, 1)
    following = to_neighbour(f, -1)

    sums = kernel_call(functools.partial(first_body, total), (4 * R, R), [f, column], meta)
    sums = add_across(0, total, with_plane_before, [f, previous], sums, meta)
    part = swap_halves(line_total(plane_scatter(sums)))
    part, following = lax.optimization_barrier((part, following))
    theirs = plane_gather(part)
    low, high = kernel_call(
        next_body, [(half, R)] * 2, [f, following, previous, theirs, coefficients, column], meta
    )

    before_high = to_neighbour(high, 1)
    after_low = to_neighbour(low, -1)
    sums, fresh = kernel_call(
        functools.partial(second_body, total),
        [(5 * R, R), (rows_here, R)],
        [low, high, f, column],
        meta,
    )
    sums = add_across(
        2 * R, total, with_half_planes, [low, high, after_low, before_high], sums, meta
    )
    mine = plane_gather(line_total(plane_scatter(sums)))
    other = swap_halves(mine)
    inverse = kernel_call(
        inverse_factor_body,
        (R, R),
        [mine],
        meta,
        [
            pltpu.VMEM((R, R), jnp.float32),
            pltpu.VMEM((B, B), jnp.float32),
            pltpu.VMEM((B // 8, 9, 8, 2 * B), jnp.float32),
            pltpu.VMEM((R, R), jnp.float32),
            pltpu.SemaphoreType.DMA(()),
        ],
        fetch=True,
    )
    basis = kernel_call(basis_body, (rows_here, R), [fresh, inverse], meta)
    other_inverse = swap_halves(inverse)
    updated = kernel_call(
        coefficient_body,
        (H, R),
        [mine, other, inverse, other_inverse, coefficients],
        meta,
        [pltpu.VMEM(mine.shape, jnp.float32)] * 2 + [pltpu.VMEM((R, R), jnp.float32)] * 2,
    )
    return (basis[None], updated)


def solution(mesh):
    torus = Mesh(mesh.devices.reshape(mesh.shape["half"], 4, 4, 4, 2), CELLS)
    return jax.shard_map(
        step,
        mesh=torus,
        in_specs=(P("half", AXES, None), P(), P(AXES)),
        out_specs=(P("half", AXES, None), P("half", None)),
        check_vma=False,
    )
```
